32 devices in a mesh: wide: 4 (over x, core), narrow: 8 (over z, y).
Axes of the slice: x: 2, y: 2, z: 4, core: 2. Of those that a mesh axis runs over, the one named last changes fastest.
Arguments:
- activations: bfloat16 [4, 32, 32, 1920], P(None, 'wide', None, 'narrow'), may hold values from -6 to 6
- covariance: float32 [17280, 17280], P('wide', 'narrow'), may hold values from -0.06 to 3, as said below
Outputs:
- updated: float32 [17280, 17280], P('wide', 'narrow')
The draws below stay inside these ranges and needn't reach their ends.
Inputs may be any that keep to these rules, and one draw needn't show every extreme that they name: `covariance`: symmetric.
All inputs are finite; a program needn't handle non-finite values.
Results may differ from the reference program's by a relative error of at most 0.0003.
Values may be sent and summed in bfloat16 or wider, within the bound.
A program may use at most 384 MiB of HBM per device.

```python
import jax
import jax.numpy as jnp
from jax import lax

C = 1920
HEIGHT = 32
WIDTH = 32
BATCH = 4
K = 17280
M = 4096


def draw_covariance(key, part):
    first = jax.random.fold_in(key, 11)
    second = jax.random.fold_in(key, 23)
    noise = jax.random.truncated_normal(first, -4.0, 4.0, (K, K), jnp.float32) * 0.01
    diagonal = jax.random.uniform(second, (K,), jnp.float32, 0.5, 1.5)
    symmetric = (noise + noise.T) * 0.7071
    positions = jnp.arange(K)
    on_diagonal = positions[:, None] == positions[None, :]
    return jnp.where(on_diagonal, diagonal[:, None], symmetric).astype(jnp.float32)


def block_scale(own_key, shape, shards, smallest, largest):
    def one(axis_at, blocks):
        draws = jax.random.uniform(jax.random.fold_in(jax.random.fold_in(own_key, 6), axis_at), (blocks,), jnp.float32, smallest / len(shards), largest / len(shards))
        return jnp.repeat(jnp.exp(draws), shape[axis_at] // blocks).reshape((-1,) + (1,) * (len(shape) - axis_at - 1))

    loudness = one(*shards[0])
    for cut in shards[1:]:
        loudness = loudness * one(*cut)
    return loudness


def gaussian(stream_key, dims, scale, reach, cuts=(), kind=jnp.bfloat16):
    values = scale * jax.random.normal(stream_key, dims, jnp.float32)
    if cuts:
        values = values * block_scale(stream_key, dims, cuts, -0.22, 0.18)
    return jnp.clip(values, -reach, reach).astype(kind)


def setup_inputs(seed: int = 0) -> dict:
    key_of = jax.random.split(jax.random.key(seed), 3)
    return {
        "activations": gaussian(key_of[0], (BATCH, HEIGHT, WIDTH, C), 1.0, 6.0, ((1, 4), (3, 8))),
        "covariance": draw_covariance(jax.random.fold_in(key_of[2], 71), 0),
    }


decay_rate = 0.9


def extract(padded, rows_out, cols_out):
    tap_views = []
    for row_tap in range(3):
        for col_tap in range(3):
            tap_views.append(padded[:, row_tap:row_tap + rows_out, col_tap:col_tap + cols_out, :])
    stacked = jnp.stack(tap_views, axis=-1)
    shape = stacked.shape
    return stacked.reshape(shape[0] * shape[1] * shape[2], shape[3] * shape[4])


def reference(activations, covariance):
    padded = jnp.pad(activations, ((0, 0), (1, 1), (1, 1), (0, 0)))
    patches = extract(padded, HEIGHT, WIDTH)
    gram = lax.dot_general(patches, patches, (((0,), (0,)), ((), ())), preferred_element_type=jnp.float32)
    return decay_rate * covariance + ((1.0 - decay_rate) / M) * gram
```

```python
import functools

import jax
import jax.numpy as jnp
from jax import lax
from jax.experimental import pallas as pl
from jax.experimental.pallas import tpu as pltpu
from jax.sharding import PartitionSpec as P

decay_rate = 0.9


def expand_kernel(width, height, image_ref, out_ref, spread):
    group, positions = image_ref.shape
    image = image_ref[...].astype(jnp.float32)
    place = lax.broadcasted_iota(jnp.int32, (8, positions), 1)
    column = place % width
    row = (place // width) % height
    row_ok = [row >= 1, None, row < height - 1]
    column_ok = [column >= 1, None, column < width - 1]
    for a in range(3):
        for b in range(3):
            offset = (a - 1) * width + (b - 1)
            moved = pltpu.roll(image, (-offset) % positions, 1) if offset else image
            keep = row_ok[a]
            if column_ok[b] is not None:
                keep = column_ok[b] if keep is None else keep & column_ok[b]
            for half in range(group // 8):
                part = moved[half * 8 : half * 8 + 8]
                if keep is not None:
                    part = jnp.where(keep, part, 0.0)
                for tile in range(positions // 128):
                    spread[tile, pl.ds(half * 72 + 3 * a + b, 8, stride=9), :] = part[
                        :, tile * 128 : tile * 128 + 128
                    ]
    for tile in range(positions // 128):
        out_ref[:, tile * 128 : tile * 128 + 128] = spread[tile].astype(jnp.bfloat16)


def expand(image, width, height):
    channels, positions = image.shape
    group = 16 if channels % 16 == 0 else 8
    return pl.pallas_call(
        functools.partial(expand_kernel, width, height),
        grid=(channels // group,),
        out_shape=jax.ShapeDtypeStruct((channels * 9, positions), jnp.bfloat16),
        in_specs=[pl.BlockSpec((group, positions), lambda i: (i, 0))],
        out_specs=pl.BlockSpec((group * 9, positions), lambda i: (i, 0)),
        scratch_shapes=[pltpu.VMEM((positions // 128, group * 9, 128), jnp.float32)],
        cost_estimate=pl.CostEstimate(
            flops=channels * 9 * positions * 20,
            bytes_accessed=channels * positions * 20,
            transcendentals=0,
        ),
    )(image)


def update_kernel(width, height, new_share, image_ref, edge_ref, patches_ref, low_ref, side_ref, covariance_ref, *rest):
    out_ref, corners, gram, spread = rest[-4:]
    group, positions = image_ref.shape
    columns = covariance_ref.shape[1]
    tiles = -(-columns // 128)
    image = image_ref[...].astype(jnp.float32)
    place = lax.broadcasted_iota(jnp.int32, (1, positions), 1)
    column = place % width
    row = (place // width) % height
    row_ok = [row >= 1, None, row < height - 1]
    column_ok = [column >= 1, None, column < width - 1]
    planes = []
    for a, b in ((0, 0), (0, 2), (2, 0), (2, 2)):
        offset = (a - 1) * width + (b - 1)
        moved = pltpu.roll(image, (-offset) % positions, 1)
        planes.append(jnp.where(row_ok[a] & column_ok[b], moved, 0.0))
    corners[...] = jnp.concatenate(planes, axis=0).astype(jnp.bfloat16)
    contract = (((1,), (1,)), ((), ()))
    gram[0 : 4 * group, 128 : 128 + columns] = lax.dot_general(
        corners[...], patches_ref[...], contract, preferred_element_type=jnp.float32
    )
    size = low_ref.shape[1]
    edge = edge_ref[...].astype(jnp.float32)
    edge = [edge[:, k * size : k * size + size] for k in (0, 2, 3, 4, 5)]
    low = lax.dot_general(
        jnp.concatenate(edge[:2], axis=0).astype(jnp.bfloat16), low_ref[...], contract, preferred_element_type=jnp.float32
    )
    gram[4 * group : 6 * group, 128 : 128 + columns] = low
    side = lax.dot_general(
        jnp.concatenate(edge[2:], axis=0).astype(jnp.bfloat16), side_ref[...], contract, preferred_element_type=jnp.float32
    )
    gram[6 * group : 9 * group, 128 : 128 + columns] = side

    def shifted(plane, tile, by):
        near = gram[plane * group : plane * group + group, tile * 128 : tile * 128 + 384]
        return pltpu.roll(near, by % 384, 1)[:, 128:256]

    for tile in range(tiles):
        tap = (lax.broadcasted_iota(jnp.int32, (1, 128), 1) + tile * 128) % 9
        here = slice(128 + tile * 128, 256 + tile * 128)
        for b in range(2):
            mine = slice((4 + b) * group, (5 + b) * group)
            gram[mine, here] = gram[mine, here] + jnp.where(
                tap < 3, shifted(2 + b, tile, -3), shifted(b, tile, 3)
            )
    first = (0, 4, 2)
    for tile in range(tiles):
        lane = lax.broadcasted_iota(jnp.int32, (1, 128), 1) + tile * 128
        here = slice(128 + tile * 128, 256 + tile * 128)
        for a in range(3):
            left = first[a]
            middle = gram[(6 + a) * group : (7 + a) * group, here] + jnp.where(
                lane % 3 == 0, shifted(left + 1, tile, -1), shifted(left, tile, 1)
            )
            taps = (
                gram[left * group : (left + 1) * group, here],
                middle,
                gram[(left + 1) * group : (left + 2) * group, here],
            )
            for b in range(3):
                spread[tile, pl.ds(3 * a + b, group, stride=9), :] = taps[b]
        end = min(columns, tile * 128 + 128)
        cut = slice(tile * 128, end)
        out_ref[:, cut] = (
            decay_rate * covariance_ref[:, cut] + new_share * spread[tile][:, : end - tile * 128]
        )


def update(image, edges, patches, low, side, covariance, group, first, steps, slabs, so_far, width, height):
    channels, positions = image.shape
    columns = covariance.shape[1]
    each = covariance.shape[0] // (9 * group * slabs)
    padded = -(-columns // 128) * 128 + 256
    whole = lambda i: (0, 0)
    once = pl.Buffered(1)
    tile = pl.BlockSpec(
        (group * 9, columns), lambda i: ((i // steps) * each + first + i % steps, 0)
    )
    operands = [image, edges, patches, low, side, covariance]
    specs = [
        pl.BlockSpec((group, positions), lambda i: (i, 0)),
        pl.BlockSpec((group, edges.shape[1]), lambda i: (i, 0)),
        pl.BlockSpec(patches.shape, whole, pipeline_mode=once),
        pl.BlockSpec(low.shape, whole, pipeline_mode=once),
        pl.BlockSpec(side.shape, whole, pipeline_mode=once),
        tile,
    ]
    aliases = {}
    if so_far is not None:
        operands.append(so_far)
        specs.append(pl.BlockSpec(memory_space=pl.ANY))
        aliases = {6: 0}
    return pl.pallas_call(
        functools.partial(update_kernel, width, height, (1.0 - decay_rate) / positions),
        grid=(slabs * steps,),
        out_shape=jax.ShapeDtypeStruct(covariance.shape, jnp.float32),
        in_specs=specs,
        out_specs=tile,
        scratch_shapes=[
            pltpu.VMEM((4 * group, positions), jnp.bfloat16),
            pltpu.VMEM((9 * group, padded), jnp.float32),
            pltpu.VMEM((-(-columns // 128), group * 9, 128), jnp.float32),
        ],
        input_output_aliases=aliases,
        cost_estimate=pl.CostEstimate(
            flops=2 * 4 * channels * positions * columns,
            bytes_accessed=channels * 9 * columns * 8 + patches.size * 2,
            transcendentals=0,
        ),
        compiler_params=pltpu.CompilerParams(vmem_limit_bytes=62 * 1024 * 1024),
    )(*operands)


def edge_selector(batch, height, width):
    place = lax.broadcasted_iota(jnp.int32, (batch * height * width, 1), 0)
    parts = []
    for size, last, stride in ((width, (height - 1) * width, 1), (height, width - 1, width)):
        line = lax.broadcasted_iota(jnp.int32, (1, batch * size), 1)
        for k in (-1, 0, 1):
            at = line % size + k
            wanted = (line // size) * height * width + last + at * stride
            parts.append((place == wanted) & (at >= 0) & (at < size))
    return jnp.concatenate(parts, axis=1).astype(jnp.bfloat16)


def edge_values(image, selector):
    return lax.dot_general(
        image, selector, (((1,), (0,)), ((), ())), preferred_element_type=jnp.float32
    ).astype(jnp.bfloat16)


def interleave(planes):
    empty = jnp.zeros_like(next(iter(planes.values())))
    stacked = jnp.stack([planes.get(t, empty) for t in range(9)], axis=1)
    return stacked.reshape(-1, stacked.shape[2])


def plain(activations, covariance):
    wide_count = lax.axis_size("wide")
    narrow_count = lax.axis_size("narrow")
    repeats = narrow_count // wide_count
    batch, rows, width, channels = activations.shape
    height = rows * wide_count
    strip = jnp.transpose(activations.reshape(batch * rows * width, channels)).reshape(
        channels, batch, rows * width
    )
    moves = []
    for r in range(wide_count):
        for s in range(narrow_count):
            target = (s // repeats) * narrow_count + r + (s % repeats) * wide_count
            moves.append((r * narrow_count + s, target))
    row_strip = lax.ppermute(strip, ("wide", "narrow"), moves)
    group = max(g for g in range(8, 49, 8) if channels % g == 0)
    steps = channels // group
    cuts = [0, (steps * 2) // 5, steps] if steps > 3 else [0, steps]
    positions = batch * height * width
    column_strips = lax.all_gather(strip, "wide")
    row_parts = []
    for low_cut, high_cut in zip(cuts[:-1], cuts[1:]):
        piece = row_strip[low_cut * group : high_cut * group]
        if row_parts:
            piece, row_parts[-1] = lax.optimization_barrier((piece, row_parts[-1]))
        row_parts.append(lax.all_gather(piece, "narrow"))
    selector = edge_selector(batch, height, width)
    column_image = jnp.transpose(column_strips, (1, 2, 0, 3)).reshape(channels, positions)
    patches = expand(column_image, width, height)
    edges = edge_values(column_image, selector)
    size = edges.shape[1] // 6
    edge = [edges[:, k * size : k * size + size] for k in range(6)]
    low = interleave({3 + b: edge[b] for b in range(3)})
    side = interleave({3 * a + 1: edge[3 + a] for a in range(3)})
    updated = None
    for part, first in enumerate(cuts[:-1]):
        count = cuts[part + 1] - first
        own = count * group
        image = jnp.transpose(
            row_parts[part].reshape(repeats, wide_count, own, batch, rows * width), (0, 2, 3, 1, 4)
        ).reshape(repeats * own, positions)
        edges = edge_values(image, selector)
        updated = update(
            image, edges, patches, low, side, covariance, group, first, count, repeats, updated, width, height
        )
    return updated


MESH = pl.DeviceIdType.MESH


def roll_taps(image, width, height):
    positions = image.shape[1]
    place = lax.broadcasted_iota(jnp.int32, (8, positions), 1)
    column = place % width
    row = (place // width) % height
    return [row >= 1, None, row < height - 1], [column >= 1, None, column < width - 1]


def gather_kernel(shape, own_ref, row_ref, patches_ref, low_ref, side_ref, sel_ref, *rest):
    (
        col, spread, staged, sel, edges, line,
        own_send, own_recv, pass_send, row_send, row_recv, local, out_sem,
    ) = rest
    width, height, wide, narrow, inner = shape
    repeats, _, batch, channels, lanes = row_ref.shape
    outer = narrow // inner
    pairs = wide // 2
    chunks = wide * batch
    positions = batch * wide * lanes
    r = lax.axis_index("wide")
    s = lax.axis_index("narrow")
    z, y = s // inner, s % inner
    pair, core = r // 2, r % 2
    sibling = pair * 2 + 1 - core
    others = [((pair + p) % pairs) * 2 + core for p in range(1, pairs)]
    steps = ((z + 1 < outer, z + 1, y), (z > 0, z - 1, y), (y + 1 < inner, z, y + 1), (y > 0, z, y - 1))

    barrier = pltpu.get_barrier_semaphore()
    for q in [sibling] + others:
        pl.semaphore_signal(barrier, inc=1, device_id=(q, s), device_id_type=MESH)
    for there, to_z, to_y in steps:

        @pl.when(there)
        def _(to_z=to_z, to_y=to_y):
            pl.semaphore_signal(barrier, inc=1, device_id=(r, to_z * inner + to_y), device_id_type=MESH)

    greeted = pairs
    for there, _, _ in steps:
        greeted = greeted + jnp.where(there, 1, 0)
    pl.semaphore_wait(barrier, greeted)

    def to_core(source, strip, q, send):
        return pltpu.make_async_remote_copy(
            src_ref=source,
            dst_ref=col.at[strip],
            send_sem=send,
            recv_sem=own_recv.at[strip],
            device_id=(q, s),
            device_id_type=MESH,
        )

    for n, q in enumerate([sibling] + others):
        to_core(own_ref, r, q, own_send.at[n]).start()
    mine = pltpu.make_async_copy(own_ref, col.at[r], local.at[repeats])
    mine.start()

    order = [r, sibling]
    for q in others:
        order += [q, (q // 2) * 2 + 1 - core]

    streams = []
    for k in range(repeats):
        source = r * repeats + k
        from_z, from_y = source // inner, source % inner
        on = y == from_y
        children = (
            (steps[0][0] & on & (z >= from_z), steps[0]),
            (steps[1][0] & on & (z <= from_z), steps[1]),
            (steps[2][0] & (y >= from_y), steps[2]),
            (steps[3][0] & (y <= from_y), steps[3]),
        )
        any_child = children[0][0] | children[1][0] | children[2][0] | children[3][0]
        streams.append((s == source, any_child, children))

    def strip_at(j):
        turn = j // 2
        other = (pair + turn) % pairs
        return other * 2 + (core + j) % 2

    def onward(k, i, source):
        j, b = i // batch, i % batch
        w = strip_at(j)
        for n, (there, (_, to_z, to_y)) in enumerate(streams[k][2]):

            @pl.when(there)
            def _(n=n, to_z=to_z, to_y=to_y):
                pltpu.make_async_remote_copy(
                    src_ref=source(w, b),
                    dst_ref=row_ref.at[k, w, b],
                    send_sem=row_send.at[k, n],
                    recv_sem=row_recv.at[k, i],
                    device_id=(r, to_z * inner + to_y),
                    device_id_type=MESH,
                ).start()

    def send_strip(j, source):
        for k in range(repeats):

            @pl.when(streams[k][0])
            def _(k=k):
                for b in range(batch):
                    onward(k, j * batch + b, source)

    from_col = lambda w, b: col.at[w, b]
    send_strip(0, lambda w, b: own_ref.at[b])

    def arrived(j):
        strip = order[j]
        to_core(col.at[strip], strip, sibling, own_send.at[0]).wait_recv()

    arrived(1)
    send_strip(1, from_col)
    for p in range(1, pairs):
        arrived(2 * p)
        to_core(col.at[order[2 * p]], order[2 * p], sibling, pass_send.at[p - 1]).start()
        send_strip(2 * p, from_col)
    for p in range(1, pairs):
        arrived(2 * p + 1)
        send_strip(2 * p + 1, from_col)
    mine.wait()
    for k in range(repeats):

        @pl.when(streams[k][0])
        def _(k=k):
            pltpu.make_async_copy(col, row_ref.at[k], local.at[k]).start()

    group = 16
    rows = group * 9
    lines = batch * height
    at = lax.broadcasted_iota(jnp.int32, (positions, 1), 0)
    across = lax.broadcasted_iota(jnp.int32, (1, batch * width), 1)
    down = lax.broadcasted_iota(jnp.int32, (1, lines), 1)
    block = height * width
    low_at = (across // width) * block + (height - 1) * width + across % width
    side_at = (down // height) * block + (down % height) * width + width - 1
    sel[...] = (at == jnp.concatenate([low_at, side_at], axis=1)).astype(jnp.float32).astype(jnp.bfloat16)
    pieces = [col[w, n] for n in range(batch) for w in range(wide)]
    edges[...] = lax.dot_general(
        jnp.concatenate(pieces, axis=1), sel[...], (((1,), (0,)), ((), ())), preferred_element_type=jnp.float32
    )
    line[...] = jnp.zeros_like(line)
    sel_copy = pltpu.make_async_copy(sel, sel_ref, local.at[repeats])
    sel_copy.start()

    def written(e, slot):
        at_row = pl.multiple_of(e * rows, 16)
        return pltpu.make_async_copy(staged.at[slot], patches_ref.at[pl.ds(at_row, rows), :], out_sem.at[slot])

    def expand_step(e):
        slot = e % 2

        @pl.when(e >= 2)
        def _():
            written(e - 2, slot).wait()

        first = pl.multiple_of(e * group, 16)
        image = jnp.concatenate(
            [col[w, n, pl.ds(first, group), :] for n in range(batch) for w in range(wide)], axis=1
        ).astype(jnp.float32)
        row_ok, column_ok = roll_taps(image, width, height)
        for a in range(3):
            for b in range(3):
                offset = (a - 1) * width + (b - 1)
                moved = pltpu.roll(image, (-offset) % positions, 1) if offset else image
                keep = row_ok[a]
                if column_ok[b] is not None:
                    keep = column_ok[b] if keep is None else keep & column_ok[b]
                for half in range(group // 8):
                    part = moved[half * 8 : half * 8 + 8]
                    if keep is not None:
                        part = jnp.where(keep, part, 0.0)
                    for tile in range(positions // 128):
                        spread[tile, pl.ds(half * 72 + 3 * a + b, 8, stride=9), :] = part[
                            :, tile * 128 : tile * 128 + 128
                        ]
        for tile in range(positions // 128):
            staged[slot, :, tile * 128 : tile * 128 + 128] = spread[tile].astype(jnp.bfloat16)
        written(e, slot).start()
        edge = edges[pl.ds(first, group), :]
        for n, (size, base, stride) in enumerate(((width, 3, 1), (height, 1, 3))):
            value = edge[:, n * batch * width : n * batch * width + batch * size]
            count = batch * size
            spot = lax.broadcasted_iota(jnp.int32, (group, count), 1) % size
            for k in (-1, 0, 1):
                moved = pltpu.roll(value, (-k) % count, 1) if k else value
                moved = jnp.where((spot + k >= 0) & (spot + k < size), moved, 0.0)
                for half in range(group // 8):
                    line[n, pl.ds(half * 72 + base + (k + 1) * stride, 8, stride=9), :] = moved[
                        half * 8 : half * 8 + 8
                    ]
        at_row = pl.multiple_of(e * rows, 16)
        low_ref[pl.ds(at_row, rows), :] = line[0].astype(jnp.bfloat16)
        side_ref[pl.ds(at_row, rows), :] = line[1].astype(jnp.bfloat16)

    expansions = channels // group

    def landed(k, i):
        ref = row_ref.at[k, strip_at(i // batch), i % batch]
        pltpu.make_async_copy(ref, ref, row_recv.at[k, i]).wait()

    def turn(i, _):
        for k in range(repeats):

            @pl.when(jnp.logical_not(streams[k][0]) & streams[k][1])
            def _(k=k):
                landed(k, i)
                onward(k, i, lambda w, b: row_ref.at[k, w, b])

        @pl.when(i < expansions)
        def _():
            expand_step(i)

        return 0

    lax.fori_loop(0, chunks, turn, 0)
    lax.fori_loop(chunks, max(chunks, expansions), lambda e, _: (expand_step(e), 0)[1], 0)
    for k in range(repeats):

        @pl.when(jnp.logical_not(streams[k][0]) & jnp.logical_not(streams[k][1]))
        def _(k=k):
            lax.fori_loop(0, chunks, lambda i, _: (landed(k, i), 0)[1], 0)

    for e in range(max(0, expansions - 2), expansions):
        written(e, e % 2).wait()
    sel_copy.wait()
    for n, q in enumerate([sibling] + others):
        to_core(own_ref, r, q, own_send.at[n]).wait_send()
    for p in range(1, pairs):
        to_core(col.at[order[2 * p]], order[2 * p], sibling, pass_send.at[p - 1]).wait_send()
    for k in range(repeats):
        for n, (there, _) in enumerate(streams[k][2]):

            @pl.when(there)
            def _(k=k, n=n):
                pltpu.make_async_copy(row_ref.at[k], row_ref.at[k], row_send.at[k, n]).wait()

        @pl.when(streams[k][0])
        def _(k=k):
            pltpu.make_async_copy(col, row_ref.at[k], local.at[k]).wait()


def gather(own, wide, narrow, width, height):
    batch, channels, lanes = own.shape
    repeats = narrow // wide
    inner = max(d for d in range(1, narrow + 1) if narrow % d == 0 and d * d <= narrow)
    positions = batch * wide * lanes
    lines = batch * (width + height)
    anywhere = pl.BlockSpec(memory_space=pl.ANY)
    vmem = pl.BlockSpec(memory_space=pltpu.VMEM)
    bf16 = jnp.bfloat16
    return pl.pallas_call(
        functools.partial(gather_kernel, (width, height, wide, narrow, inner)),
        out_shape=[
            jax.ShapeDtypeStruct((repeats, wide, batch, channels, lanes), bf16),
            jax.ShapeDtypeStruct((channels * 9, positions), bf16),
            jax.ShapeDtypeStruct((channels * 9, batch * width), bf16),
            jax.ShapeDtypeStruct((channels * 9, batch * height), bf16),
            jax.ShapeDtypeStruct((positions, lines), bf16),
        ],
        in_specs=[vmem],
        out_specs=[anywhere, anywhere, vmem, vmem, anywhere],
        scratch_shapes=[
            pltpu.VMEM((wide, batch, channels, lanes), bf16),
            pltpu.VMEM((positions // 128, 144, 128), jnp.float32),
            pltpu.VMEM((2, 144, positions), bf16),
            pltpu.VMEM((positions, lines), bf16),
            pltpu.VMEM((channels, lines), jnp.float32),
            pltpu.VMEM((2, 144, batch * width), jnp.float32),
            pltpu.SemaphoreType.DMA((wide // 2,)),
            pltpu.SemaphoreType.DMA((wide,)),
            pltpu.SemaphoreType.DMA((max(1, wide // 2 - 1),)),
            pltpu.SemaphoreType.DMA((repeats, 4)),
            pltpu.SemaphoreType.DMA((repeats, wide * batch)),
            pltpu.SemaphoreType.DMA((repeats + 1,)),
            pltpu.SemaphoreType.DMA((2,)),
        ],
        compiler_params=pltpu.CompilerParams(
            collective_id=0, has_side_effects=True, vmem_limit_bytes=60 * 1024 * 1024
        ),
    )(own)


def combine_kernel(width, height, new_share, row_ref, patches_ref, low_ref, side_ref, sel_ref, covariance_ref, out_ref, edges, corners, gram, spread):
    repeats, wide, batch, channels, lanes = row_ref.shape
    positions = wide * batch * lanes
    group = corners.shape[0] // 4
    steps = channels // group
    columns = covariance_ref.shape[1]
    tiles = -(-columns // 128)
    step = pl.program_id(0)
    k = step // steps
    first = pl.multiple_of((step % steps) * group, 8)
    size = low_ref.shape[1]
    down = side_ref.shape[1]
    contract = (((1,), (1,)), ((), ()))

    @pl.when(step == 0)
    def _():
        for k in range(repeats):
            whole = jnp.concatenate([row_ref[k, w, n] for n in range(batch) for w in range(wide)], axis=1)
            edges[k] = lax.dot_general(
                whole, sel_ref[...], (((1,), (0,)), ((), ())), preferred_element_type=jnp.float32
            )

    image = jnp.concatenate(
        [row_ref[k, w, n, pl.ds(first, group), :] for n in range(batch) for w in range(wide)], axis=1
    ).astype(jnp.float32)
    place = lax.broadcasted_iota(jnp.int32, (1, positions), 1)
    column = place % width
    row = (place // width) % height
    row_ok = [row >= 1, None, row < height - 1]
    column_ok = [column >= 1, None, column < width - 1]
    for n, (a, b) in enumerate(((0, 0), (0, 2), (2, 0), (2, 2))):
        offset = (a - 1) * width + (b - 1)
        moved = pltpu.roll(image, (-offset) % positions, 1)
        moved = jnp.where(row_ok[a] & column_ok[b], moved, 0.0)
        corners[n * group : n * group + group, :] = moved.astype(jnp.bfloat16)
    gram[0 : 4 * group, 128 : 128 + columns] = lax.dot_general(
        corners[...], patches_ref[...], contract, preferred_element_type=jnp.float32
    )
    edge = edges[k, pl.ds(first, group), :]

    def edge_taps(value, length, taps):
        count = value.shape[1]
        spot = lax.broadcasted_iota(jnp.int32, value.shape, 1) % length
        out = []
        for by in taps:
            moved = pltpu.roll(value, (-by) % count, 1) if by else value
            out.append(jnp.where((spot + by >= 0) & (spot + by < length), moved, 0.0))
        return jnp.concatenate(out, axis=0).astype(jnp.bfloat16)

    gram[4 * group : 6 * group, 128 : 128 + columns] = lax.dot_general(
        edge_taps(edge[:, :size], width, (-1, 1)), low_ref[...], contract, preferred_element_type=jnp.float32
    )
    gram[6 * group : 9 * group, 128 : 128 + columns] = lax.dot_general(
        edge_taps(edge[:, size : size + down], height, (-1, 0, 1)), side_ref[...], contract, preferred_element_type=jnp.float32
    )

    def shifted(plane, tile, by):
        near = gram[plane * group : plane * group + group, tile * 128 : tile * 128 + 384]
        return pltpu.roll(near, by % 384, 1)[:, 128:256]

    for tile in range(tiles):
        tap = (lax.broadcasted_iota(jnp.int32, (1, 128), 1) + tile * 128) % 9
        here = slice(128 + tile * 128, 256 + tile * 128)
        for b in range(2):
            mine = slice((4 + b) * group, (5 + b) * group)
            gram[mine, here] = gram[mine, here] + jnp.where(
                tap < 3, shifted(2 + b, tile, -3), shifted(b, tile, 3)
            )
    starts = (0, 4, 2)
    for tile in range(tiles):
        lane = lax.broadcasted_iota(jnp.int32, (1, 128), 1) + tile * 128
        here = slice(128 + tile * 128, 256 + tile * 128)
        slot = tile % 2
        for a in range(3):
            left = starts[a]
            middle = gram[(6 + a) * group : (7 + a) * group, here] + jnp.where(
                lane % 3 == 0, shifted(left + 1, tile, -1), shifted(left, tile, 1)
            )
            taps = (
                gram[left * group : (left + 1) * group, here],
                middle,
                gram[(left + 1) * group : (left + 2) * group, here],
            )
            for b in range(3):
                spread[slot, pl.ds(3 * a + b, group, stride=9), :] = taps[b]
        end = min(columns, tile * 128 + 128)
        cut = slice(tile * 128, end)
        out_ref[:, cut] = (
            decay_rate * covariance_ref[:, cut] + new_share * spread[slot][:, : end - tile * 128]
        )


def combine(row, patches, low, side, sel, covariance, width, height):
    repeats, wide, batch, channels, lanes = row.shape
    positions = wide * batch * lanes
    columns = covariance.shape[1]
    group = max(g for g in range(8, 49, 8) if channels % g == 0)
    steps = channels // group
    padded = -(-columns // 128) * 128 + 256
    once = pl.Buffered(1)

    def resident(array):
        return pl.BlockSpec(array.shape, lambda i: (0,) * array.ndim, pipeline_mode=once)

    tile = pl.BlockSpec((group * 9, columns), lambda i: (i, 0))
    return pl.pallas_call(
        functools.partial(combine_kernel, width, height, (1.0 - decay_rate) / positions),
        grid=(repeats * steps,),
        out_shape=jax.ShapeDtypeStruct(covariance.shape, jnp.float32),
        in_specs=[resident(a) for a in (row, patches, low, side, sel)] + [tile],
        out_specs=tile,
        scratch_shapes=[
            pltpu.VMEM((repeats, channels, sel.shape[1]), jnp.float32),
            pltpu.VMEM((4 * group, positions), jnp.bfloat16),
            pltpu.VMEM((9 * group, padded), jnp.float32),
            pltpu.VMEM((2, group * 9, 128), jnp.float32),
        ],
        cost_estimate=pl.CostEstimate(
            flops=2 * 4 * repeats * channels * positions * columns,
            bytes_accessed=covariance.size * 8 + patches.size * 2,
            transcendentals=0,
        ),
        compiler_params=pltpu.CompilerParams(vmem_limit_bytes=62 * 1024 * 1024),
    )(row, patches, low, side, sel, covariance)


def shards(activations, covariance):
    wide = lax.axis_size("wide")
    narrow = lax.axis_size("narrow")
    batch, rows, width, channels = activations.shape
    height = rows * wide
    lanes = rows * width
    if lanes % 128 or channels % 16 or wide % 2 or narrow % wide or width != height:
        return plain(activations, covariance)
    own = jnp.transpose(activations.reshape(batch, lanes, channels), (0, 2, 1))
    row, patches, low, side, sel = gather(own, wide, narrow, width, height)
    return combine(row, patches, low, side, sel, covariance, width, height)


def solution(mesh):
    return jax.shard_map(
        shards,
        mesh=mesh,
        in_specs=(P(None, "wide", None, "narrow"), P("wide", "narrow")),
        out_specs=P("wide", "narrow"),
        check_vma=False,
    )
```

```python
import functools

import jax
import jax.numpy as jnp
from jax import lax
from jax.experimental import pallas as pl
from jax.experimental.pallas import tpu as pltpu
from jax.sharding import PartitionSpec as P

decay_rate = 0.9


def expand_kernel(width, height, image_ref, out_ref, spread):
    group, positions = image_ref.shape
    image = image_ref[...].astype(jnp.float32)
    place = lax.broadcasted_iota(jnp.int32, (8, positions), 1)
    column = place % width
    row = (place // width) % height
    row_ok = [row >= 1, None, row < height - 1]
    column_ok = [column >= 1, None, column < width - 1]
    for a in range(3):
        for b in range(3):
            offset = (a - 1) * width + (b - 1)
            moved = pltpu.roll(image, (-offset) % positions, 1) if offset else image
            keep = row_ok[a]
            if column_ok[b] is not None:
                keep = column_ok[b] if keep is None else keep & column_ok[b]
            for half in range(group // 8):
                part = moved[half * 8 : half * 8 + 8]
                if keep is not None:
                    part = jnp.where(keep, part, 0.0)
                for tile in range(positions // 128):
                    spread[tile, pl.ds(half * 72 + 3 * a + b, 8, stride=9), :] = part[
                        :, tile * 128 : tile * 128 + 128
                    ]
    for tile in range(positions // 128):
        out_ref[:, tile * 128 : tile * 128 + 128] = spread[tile].astype(jnp.bfloat16)


def expand(image, width, height):
    channels, positions = image.shape
    group = 16 if channels % 16 == 0 else 8
    return pl.pallas_call(
        functools.partial(expand_kernel, width, height),
        grid=(channels // group,),
        out_shape=jax.ShapeDtypeStruct((channels * 9, positions), jnp.bfloat16),
        in_specs=[pl.BlockSpec((group, positions), lambda i: (i, 0))],
        out_specs=pl.BlockSpec((group * 9, positions), lambda i: (i, 0)),
        scratch_shapes=[pltpu.VMEM((positions // 128, group * 9, 128), jnp.float32)],
        cost_estimate=pl.CostEstimate(
            flops=channels * 9 * positions * 20,
            bytes_accessed=channels * positions * 20,
            transcendentals=0,
        ),
    )(image)


def update_kernel(width, height, new_share, image_ref, edge_ref, patches_ref, low_ref, side_ref, covariance_ref, *rest):
    out_ref, corners, gram, spread = rest[-4:]
    group, positions = image_ref.shape
    columns = covariance_ref.shape[1]
    tiles = -(-columns // 128)
    image = image_ref[...].astype(jnp.float32)
    place = lax.broadcasted_iota(jnp.int32, (1, positions), 1)
    column = place % width
    row = (place // width) % height
    row_ok = [row >= 1, None, row < height - 1]
    column_ok = [column >= 1, None, column < width - 1]
    planes = []
    for a, b in ((0, 0), (0, 2), (2, 0), (2, 2)):
        offset = (a - 1) * width + (b - 1)
        moved = pltpu.roll(image, (-offset) % positions, 1)
        planes.append(jnp.where(row_ok[a] & column_ok[b], moved, 0.0))
    corners[...] = jnp.concatenate(planes, axis=0).astype(jnp.bfloat16)
    contract = (((1,), (1,)), ((), ()))
    gram[0 : 4 * group, 128 : 128 + columns] = lax.dot_general(
        corners[...], patches_ref[...], contract, preferred_element_type=jnp.float32
    )
    size = low_ref.shape[1]
    edge = edge_ref[...].astype(jnp.float32)
    edge = [edge[:, k * size : k * size + size] for k in (0, 2, 3, 4, 5)]
    low = lax.dot_general(
        jnp.concatenate(edge[:2], axis=0).astype(jnp.bfloat16), low_ref[...], contract, preferred_element_type=jnp.float32
    )
    gram[4 * group : 6 * group, 128 : 128 + columns] = low
    side = lax.dot_general(
        jnp.concatenate(edge[2:], axis=0).astype(jnp.bfloat16), side_ref[...], contract, preferred_element_type=jnp.float32
    )
    gram[6 * group : 9 * group, 128 : 128 + columns] = side

    def shifted(plane, tile, by):
        near = gram[plane * group : plane * group + group, tile * 128 : tile * 128 + 384]
        return pltpu.roll(near, by % 384, 1)[:, 128:256]

    for tile in range(tiles):
        tap = (lax.broadcasted_iota(jnp.int32, (1, 128), 1) + tile * 128) % 9
        here = slice(128 + tile * 128, 256 + tile * 128)
        for b in range(2):
            mine = slice((4 + b) * group, (5 + b) * group)
            gram[mine, here] = gram[mine, here] + jnp.where(
                tap < 3, shifted(2 + b, tile, -3), shifted(b, tile, 3)
            )
    first = (0, 4, 2)
    for tile in range(tiles):
        lane = lax.broadcasted_iota(jnp.int32, (1, 128), 1) + tile * 128
        here = slice(128 + tile * 128, 256 + tile * 128)
        for a in range(3):
            left = first[a]
            middle = gram[(6 + a) * group : (7 + a) * group, here] + jnp.where(
                lane % 3 == 0, shifted(left + 1, tile, -1), shifted(left, tile, 1)
            )
            taps = (
                gram[left * group : (left + 1) * group, here],
                middle,
                gram[(left + 1) * group : (left + 2) * group, here],
            )
            for b in range(3):
                spread[tile, pl.ds(3 * a + b, group, stride=9), :] = taps[b]
        end = min(columns, tile * 128 + 128)
        cut = slice(tile * 128, end)
        out_ref[:, cut] = (
            decay_rate * covariance_ref[:, cut] + new_share * spread[tile][:, : end - tile * 128]
        )


def update(image, edges, patches, low, side, covariance, group, first, steps, slabs, so_far, width, height):
    channels, positions = image.shape
    columns = covariance.shape[1]
    each = covariance.shape[0] // (9 * group * slabs)
    padded = -(-columns // 128) * 128 + 256
    whole = lambda i: (0, 0)
    once = pl.Buffered(1)
    tile = pl.BlockSpec(
        (group * 9, columns), lambda i: ((i // steps) * each + first + i % steps, 0)
    )
    operands = [image, edges, patches, low, side, covariance]
    specs = [
        pl.BlockSpec((group, positions), lambda i: (i, 0)),
        pl.BlockSpec((group, edges.shape[1]), lambda i: (i, 0)),
        pl.BlockSpec(patches.shape, whole, pipeline_mode=once),
        pl.BlockSpec(low.shape, whole, pipeline_mode=once),
        pl.BlockSpec(side.shape, whole, pipeline_mode=once),
        tile,
    ]
    aliases = {}
    if so_far is not None:
        operands.append(so_far)
        specs.append(pl.BlockSpec(memory_space=pl.ANY))
        aliases = {6: 0}
    return pl.pallas_call(
        functools.partial(update_kernel, width, height, (1.0 - decay_rate) / positions),
        grid=(slabs * steps,),
        out_shape=jax.ShapeDtypeStruct(covariance.shape, jnp.float32),
        in_specs=specs,
        out_specs=tile,
        scratch_shapes=[
            pltpu.VMEM((4 * group, positions), jnp.bfloat16),
            pltpu.VMEM((9 * group, padded), jnp.float32),
            pltpu.VMEM((-(-columns // 128), group * 9, 128), jnp.float32),
        ],
        input_output_aliases=aliases,
        cost_estimate=pl.CostEstimate(
            flops=2 * 4 * channels * positions * columns,
            bytes_accessed=channels * 9 * columns * 8 + patches.size * 2,
            transcendentals=0,
        ),
        compiler_params=pltpu.CompilerParams(vmem_limit_bytes=62 * 1024 * 1024),
    )(*operands)


def edge_selector(batch, height, width):
    place = lax.broadcasted_iota(jnp.int32, (batch * height * width, 1), 0)
    parts = []
    for size, last, stride in ((width, (height - 1) * width, 1), (height, width - 1, width)):
        line = lax.broadcasted_iota(jnp.int32, (1, batch * size), 1)
        for k in (-1, 0, 1):
            at = line % size + k
            wanted = (line // size) * height * width + last + at * stride
            parts.append((place == wanted) & (at >= 0) & (at < size))
    return jnp.concatenate(parts, axis=1).astype(jnp.bfloat16)


def edge_values(image, selector):
    return lax.dot_general(
        image, selector, (((1,), (0,)), ((), ())), preferred_element_type=jnp.float32
    ).astype(jnp.bfloat16)


def interleave(planes):
    empty = jnp.zeros_like(next(iter(planes.values())))
    stacked = jnp.stack([planes.get(t, empty) for t in range(9)], axis=1)
    return stacked.reshape(-1, stacked.shape[2])


def plain(activations, covariance):
    wide_count = lax.axis_size("wide")
    narrow_count = lax.axis_size("narrow")
    repeats = narrow_count // wide_count
    batch, rows, width, channels = activations.shape
    height = rows * wide_count
    strip = jnp.transpose(activations.reshape(batch * rows * width, channels)).reshape(
        channels, batch, rows * width
    )
    moves = []
    for r in range(wide_count):
        for s in range(narrow_count):
            target = (s // repeats) * narrow_count + r + (s % repeats) * wide_count
            moves.append((r * narrow_count + s, target))
    row_strip = lax.ppermute(strip, ("wide", "narrow"), moves)
    group = max(g for g in range(8, 49, 8) if channels % g == 0)
    steps = channels // group
    cuts = [0, (steps * 2) // 5, steps] if steps > 3 else [0, steps]
    positions = batch * height * width
    column_strips = lax.all_gather(strip, "wide")
    row_parts = []
    for low_cut, high_cut in zip(cuts[:-1], cuts[1:]):
        piece = row_strip[low_cut * group : high_cut * group]
        if row_parts:
            piece, row_parts[-1] = lax.optimization_barrier((piece, row_parts[-1]))
        row_parts.append(lax.all_gather(piece, "narrow"))
    selector = edge_selector(batch, height, width)
    column_image = jnp.transpose(column_strips, (1, 2, 0, 3)).reshape(channels, positions)
    patches = expand(column_image, width, height)
    edges = edge_values(column_image, selector)
    size = edges.shape[1] // 6
    edge = [edges[:, k * size : k * size + size] for k in range(6)]
    low = interleave({3 + b: edge[b] for b in range(3)})
    side = interleave({3 * a + 1: edge[3 + a] for a in range(3)})
    updated = None
    for part, first in enumerate(cuts[:-1]):
        count = cuts[part + 1] - first
        own = count * group
        image = jnp.transpose(
            row_parts[part].reshape(repeats, wide_count, own, batch, rows * width), (0, 2, 3, 1, 4)
        ).reshape(repeats * own, positions)
        edges = edge_values(image, selector)
        updated = update(
            image, edges, patches, low, side, covariance, group, first, count, repeats, updated, width, height
        )
    return updated


MESH = pl.DeviceIdType.MESH


def roll_taps(image, width, height):
    positions = image.shape[1]
    place = lax.broadcasted_iota(jnp.int32, (8, positions), 1)
    column = place % width
    row = (place // width) % height
    return [row >= 1, None, row < height - 1], [column >= 1, None, column < width - 1]


def gather_kernel(shape, own_ref, row_ref, patches_ref, low_ref, side_ref, sel_ref, *rest):
    (
        col, spread, staged, sel, edges, line,
        own_send, own_recv, pass_send, row_send, row_recv, local, out_sem,
    ) = rest
    width, height, wide, narrow, inner = shape
    repeats, _, batch, channels, lanes = row_ref.shape
    outer = narrow // inner
    pairs = wide // 2
    r = lax.axis_index("wide")
    s = lax.axis_index("narrow")
    z, y = s // inner, s % inner
    pair, core = r // 2, r % 2
    sibling = pair * 2 + 1 - core
    others = [((pair + p) % pairs) * 2 + core for p in range(1, pairs)]
    steps = ((z + 1 < outer, z + 1, y), (z > 0, z - 1, y), (y + 1 < inner, z, y + 1), (y > 0, z, y - 1))

    barrier = pltpu.get_barrier_semaphore()
    for q in [sibling] + others:
        pl.semaphore_signal(barrier, inc=1, device_id=(q, s), device_id_type=MESH)
    for there, to_z, to_y in steps:

        @pl.when(there)
        def _(to_z=to_z, to_y=to_y):
            pl.semaphore_signal(barrier, inc=1, device_id=(r, to_z * inner + to_y), device_id_type=MESH)

    greeted = pairs
    for there, _, _ in steps:
        greeted = greeted + jnp.where(there, 1, 0)
    pl.semaphore_wait(barrier, greeted)

    def to_core(source, strip, b, q, send):
        return pltpu.make_async_remote_copy(
            src_ref=source,
            dst_ref=col.at[strip, b],
            send_sem=send,
            recv_sem=own_recv.at[strip, b],
            device_id=(q, s),
            device_id_type=MESH,
        )

    def first_sends(b):
        return [to_core(own_ref.at[b], r, b, q, own_send.at[n, b]) for n, q in enumerate([sibling] + others)]

    for b in range(batch):
        for copy in first_sends(b):
            copy.start()
    mine = pltpu.make_async_copy(own_ref, col.at[r], local.at[repeats])
    mine.start()

    order = [r, sibling]
    for q in others:
        order += [q, (q // 2) * 2 + 1 - core]

    streams = []
    for k in range(repeats):
        source = r * repeats + k
        from_z, from_y = source // inner, source % inner
        on = y == from_y
        children = (
            (steps[0][0] & on & (z >= from_z), steps[0]),
            (steps[1][0] & on & (z <= from_z), steps[1]),
            (steps[2][0] & (y >= from_y), steps[2]),
            (steps[3][0] & (y <= from_y), steps[3]),
        )
        any_child = children[0][0] | children[1][0] | children[2][0] | children[3][0]
        streams.append((s == source, any_child, children))

    def onward(k, j, b, source):
        for n, (there, (_, to_z, to_y)) in enumerate(streams[k][2]):

            @pl.when(there)
            def _(n=n, to_z=to_z, to_y=to_y):
                pltpu.make_async_remote_copy(
                    src_ref=source,
                    dst_ref=row_ref.at[k, order[j], b],
                    send_sem=row_send.at[k, n],
                    recv_sem=row_recv.at[k, j, b],
                    device_id=(r, to_z * inner + to_y),
                    device_id_type=MESH,
                ).start()

    def landed(k, j, b):
        ref = row_ref.at[k, order[j], b]
        pltpu.make_async_copy(ref, ref, row_recv.at[k, j, b]).wait()

    def passed(p, b):
        strip = order[2 * p]
        return to_core(col.at[strip, b], strip, b, sibling, pass_send.at[p - 1, b])

    group = 16
    rows = group * 9
    expansions = channels // group
    share = -(-expansions // wide)
    block = height * width
    positions = batch * block
    lines = batch * height
    at = lax.broadcasted_iota(jnp.int32, (1, positions), 1)
    across = lax.broadcasted_iota(jnp.int32, (batch * width, 1), 0)
    down = lax.broadcasted_iota(jnp.int32, (lines, 1), 0)
    low_at = (across // width) * block + (height - 1) * width + across % width
    side_at = (down // height) * block + (down % height) * width + width - 1
    for n, wanted in enumerate((low_at, side_at)):
        sel[n * batch * width : n * batch * width + wanted.shape[0], :] = (
            (at == wanted).astype(jnp.float32).astype(jnp.bfloat16)
        )
    sel_copy = pltpu.make_async_copy(sel, sel_ref, local.at[repeats + 1])
    sel_copy.start()
    line[...] = jnp.zeros_like(line)
    for ref in (low_ref, side_ref):
        ref[channels * 9 :, :] = jnp.zeros((ref.shape[0] - channels * 9, ref.shape[1]), jnp.bfloat16)

    def written(e, b, slot):
        top = pl.multiple_of(e * rows, 16)
        left = pl.multiple_of(b * block, 128)
        return pltpu.make_async_copy(
            staged.at[slot], patches_ref.at[pl.ds(top, rows), pl.ds(left, block)], out_sem.at[slot]
        )

    def expand_step(e, b):
        turn = b * expansions + e
        slot = turn % 2

        @pl.when(turn >= 2)
        def _():
            written(0, 0, slot).wait()

        first = pl.multiple_of(e * group, 16)
        image = jnp.concatenate([col[w, b, pl.ds(first, group), :] for w in range(wide)], axis=1).astype(jnp.float32)
        row_ok, column_ok = roll_taps(image, width, height)
        for a in range(3):
            for c in range(3):
                offset = (a - 1) * width + (c - 1)
                moved = pltpu.roll(image, (-offset) % block, 1) if offset else image
                keep = row_ok[a]
                if column_ok[c] is not None:
                    keep = column_ok[c] if keep is None else keep & column_ok[c]
                for half in range(group // 8):
                    part = moved[half * 8 : half * 8 + 8]
                    if keep is not None:
                        part = jnp.where(keep, part, 0.0)
                    for tile in range(block // 128):
                        spread[tile, pl.ds(half * 72 + 3 * a + c, 8, stride=9), :] = part[
                            :, tile * 128 : tile * 128 + 128
                        ]
        for tile in range(block // 128):
            staged[slot, :, tile * 128 : tile * 128 + 128] = spread[tile].astype(jnp.bfloat16)
        written(e, b, slot).start()

    mine.wait()

    def turn(b, _):
        for j in range(wide):
            if j > 0:
                to_core(col.at[order[j], b], order[j], b, sibling, own_send.at[0, b]).wait_recv()
            if j > 1 and j % 2 == 0:
                passed(j // 2, b).start()
            for k in range(repeats):

                @pl.when(streams[k][0])
                def _(k=k):
                    onward(k, j, b, col.at[order[j], b])

        for j in range(wide):
            for k in range(repeats):

                @pl.when(jnp.logical_not(streams[k][0]) & streams[k][1])
                def _(k=k):
                    landed(k, j, b)
                    onward(k, j, b, row_ref.at[k, order[j], b])

            @pl.when(b > 0)
            def _(j=j):
                lax.fori_loop(
                    j * share, min(expansions, j * share + share), lambda e, _: (expand_step(e, b - 1), 0)[1], 0
                )

        return 0

    lax.fori_loop(0, batch, turn, 0)
    for k in range(repeats):

        @pl.when(streams[k][0])
        def _(k=k):
            pltpu.make_async_copy(col, row_ref.at[k], local.at[k]).start()

    lax.fori_loop(0, expansions, lambda e, _: (expand_step(e, batch - 1), 0)[1], 0)
    pieces = [col[w, n] for n in range(batch) for w in range(wide)]
    edges[...] = lax.dot_general(
        jnp.concatenate(pieces, axis=1), sel[...], (((1,), (1,)), ((), ())), preferred_element_type=jnp.float32
    )

    def edge_step(e, _):
        first = pl.multiple_of(e * group, 16)
        edge = edges[pl.ds(first, group), :]
        for n, (size, base, stride) in enumerate(((width, 3, 1), (height, 1, 3))):
            count = batch * size
            value = edge[:, n * batch * width : n * batch * width + count]
            spot = lax.broadcasted_iota(jnp.int32, (group, count), 1) % size
            for k in (-1, 0, 1):
                moved = pltpu.roll(value, (-k) % count, 1) if k else value
                moved = jnp.where((spot + k >= 0) & (spot + k < size), moved, 0.0)
                for half in range(group // 8):
                    line[n, pl.ds(half * 72 + base + (k + 1) * stride, 8, stride=9), :] = moved[
                        half * 8 : half * 8 + 8
                    ]
        top = pl.multiple_of(e * rows, 16)
        low_ref[pl.ds(top, rows), :] = line[0].astype(jnp.bfloat16)
        side_ref[pl.ds(top, rows), :] = line[1].astype(jnp.bfloat16)
        return 0

    lax.fori_loop(0, expansions, edge_step, 0)
    for k in range(repeats):

        @pl.when(jnp.logical_not(streams[k][0]) & jnp.logical_not(streams[k][1]))
        def _(k=k):
            for b in range(batch):
                for j in range(wide):
                    landed(k, j, b)

    for slot in range(min(2, batch * expansions)):
        written(0, 0, slot).wait()
    sel_copy.wait()
    for b in range(batch):
        for copy in first_sends(b):
            copy.wait_send()
        for p in range(1, pairs):
            passed(p, b).wait_send()
    for k in range(repeats):
        for n, (there, _) in enumerate(streams[k][2]):

            @pl.when(there)
            def _(k=k, n=n):
                pltpu.make_async_copy(row_ref.at[k], row_ref.at[k], row_send.at[k, n]).wait()

        @pl.when(streams[k][0])
        def _(k=k):
            pltpu.make_async_copy(col, row_ref.at[k], local.at[k]).wait()


def gather(own, wide, narrow, width, height):
    batch, channels, lanes = own.shape
    repeats = narrow // wide
    inner = max(d for d in range(1, narrow + 1) if narrow % d == 0 and d * d <= narrow)
    positions = batch * wide * lanes
    lines = batch * (width + height)
    padded = padded_columns(channels * 9)
    anywhere = pl.BlockSpec(memory_space=pl.ANY)
    vmem = pl.BlockSpec(memory_space=pltpu.VMEM)
    bf16 = jnp.bfloat16
    return pl.pallas_call(
        functools.partial(gather_kernel, (width, height, wide, narrow, inner)),
        out_shape=[
            jax.ShapeDtypeStruct((repeats, wide, batch, channels, lanes), bf16),
            jax.ShapeDtypeStruct((channels * 9, positions), bf16),
            jax.ShapeDtypeStruct((padded, batch * width), bf16),
            jax.ShapeDtypeStruct((padded, batch * height), bf16),
            jax.ShapeDtypeStruct((lines, positions), bf16),
        ],
        in_specs=[vmem],
        out_specs=[anywhere, anywhere, vmem, vmem, anywhere],
        scratch_shapes=[
            pltpu.VMEM((wide, batch, channels, lanes), bf16),
            pltpu.VMEM((wide * lanes // 128, 144, 128), jnp.float32),
            pltpu.VMEM((2, 144, wide * lanes), bf16),
            pltpu.VMEM((lines, positions), bf16),
            pltpu.VMEM((channels, lines), jnp.float32),
            pltpu.VMEM((2, 144, batch * width), jnp.float32),
            pltpu.SemaphoreType.DMA((wide // 2, batch)),
            pltpu.SemaphoreType.DMA((wide, batch)),
            pltpu.SemaphoreType.DMA((max(1, wide // 2 - 1), batch)),
            pltpu.SemaphoreType.DMA((repeats, 4)),
            pltpu.SemaphoreType.DMA((repeats, wide, batch)),
            pltpu.SemaphoreType.DMA((repeats + 2,)),
            pltpu.SemaphoreType.DMA((2,)),
        ],
        compiler_params=pltpu.CompilerParams(
            collective_id=0, has_side_effects=True, vmem_limit_bytes=60 * 1024 * 1024
        ),
    )(own)


parts = 3


def padded_columns(columns):
    return -(-columns // (256 * parts)) * 256 * parts


def combine_kernel(
    width, height, new_share, row_ref, low_ref, side_ref, sel_ref, patches_ref, covariance_ref, out_ref,
    patches, edges, corners, low_rows, side_rows, even, odd, rolled, spread, fetched,
):
    repeats, wide, batch, channels, lanes = row_ref.shape
    positions = wide * batch * lanes
    group = corners.shape[0] // 4
    steps = channels // group
    groups = repeats * steps
    sub = group // parts
    columns = covariance_ref.shape[1]
    tiles = -(-columns // 128)
    chunk = patches.shape[0] // parts
    at = pl.program_id(0)
    i, j = at // parts, at % parts
    size = low_ref.shape[1]
    lines = sel_ref.shape[0]
    contract = (((1,), (1,)), ((), ()))

    pieces = [n for n in range(parts) if n * chunk < columns]

    def fetch(n):
        rows = pl.ds(n * chunk, min(chunk, columns - n * chunk))
        return pltpu.make_async_copy(patches_ref.at[rows, :], patches.at[rows, :], fetched.at[n])

    selector = pltpu.make_async_copy(sel_ref, corners.at[pl.ds(0, lines), :], fetched.at[parts])

    @pl.when(at == 0)
    def _():
        selector.start()
        for n in pieces:
            fetch(n).start()
        patches[columns:, :] = jnp.zeros((patches.shape[0] - columns, positions), jnp.bfloat16)
        selector.wait()
        for k in range(repeats):
            whole = jnp.concatenate([row_ref[k, w, n] for n in range(batch) for w in range(wide)], axis=1)
            edges[k] = lax.dot_general(whole, corners[0:lines, :], contract, preferred_element_type=jnp.float32)

    def edge_taps(value, length, taps):
        count = value.shape[1]
        spot = lax.broadcasted_iota(jnp.int32, value.shape, 1) % length
        out = []
        for by in taps:
            moved = pltpu.roll(value, (-by) % count, 1) if by else value
            out.append(jnp.where((spot + by >= 0) & (spot + by < length), moved, 0.0))
        return jnp.concatenate(out, axis=0).astype(jnp.bfloat16)

    @pl.when((j == 0) & (i < groups))
    def _():
        k = i // steps
        first = pl.multiple_of((i % steps) * group, 8)
        image = jnp.concatenate(
            [row_ref[k, w, n, pl.ds(first, group), :] for n in range(batch) for w in range(wide)], axis=1
        ).astype(jnp.float32)
        place = lax.broadcasted_iota(jnp.int32, (1, positions), 1)
        column = place % width
        row = (place // width) % height
        row_ok = [row >= 1, None, row < height - 1]
        column_ok = [column >= 1, None, column < width - 1]
        for n, (a, b) in enumerate(((0, 0), (0, 2), (2, 0), (2, 2))):
            offset = (a - 1) * width + (b - 1)
            moved = pltpu.roll(image, (-offset) % positions, 1)
            moved = jnp.where(row_ok[a] & column_ok[b], moved, 0.0)
            corners[n * group : n * group + group, :] = moved.astype(jnp.bfloat16)
        edge = edges[k, pl.ds(first, group), :]
        low_rows[...] = edge_taps(edge[:, :size], width, (-1, 1))
        side_rows[...] = edge_taps(edge[:, size:], height, (-1, 0, 1))

    for n in pieces:

        @pl.when(at == n)
        def _(n=n):
            fetch(n).wait()

    def multiply(gram):
        for piece in range(chunk // 256):
            start = pl.multiple_of(j * chunk + piece * 256, 256)
            here = pl.ds(pl.multiple_of(128 + start, 128), 256)
            rows = pl.ds(start, 256)
            for left, right, top, count in (
                (corners, patches, 0, 4),
                (low_rows, low_ref, 4, 2),
                (side_rows, side_ref, 6, 3),
            ):
                gram[top * group : (top + count) * group, here] = lax.dot_general(
                    left[...], right[rows, :], contract, preferred_element_type=jnp.float32
                )

    lane = lax.broadcasted_iota(jnp.int32, (8, 128), 1)

    def finish(gram):
        def rows_of(p, n):
            return pl.ds(pl.multiple_of(p * group + j * sub + n * 8, 8), 8)

        def place(tile):
            return slice(128 + tile * 128, 256 + tile * 128)

        def roll_all(n, wanted):
            for q, p, by in wanted:
                for tile in range(tiles):
                    rolled[n % 2, q, :, tile * 128 : tile * 128 + 128] = pltpu.roll(
                        gram[rows_of(p, n), place(tile)], by % 128, 1
                    )

        def from_left(n, q, tile, by):
            here = rolled[n % 2, q, :, tile * 128 : tile * 128 + 128]
            if tile == 0:
                return here
            return jnp.where(lane < by, rolled[n % 2, q, :, tile * 128 - 128 : tile * 128], here)

        def from_right(n, q, tile, by):
            here = rolled[n % 2, q, :, tile * 128 : tile * 128 + 128]
            if tile == tiles - 1:
                return here
            return jnp.where(lane >= 128 - by, rolled[n % 2, q, :, tile * 128 + 128 : tile * 128 + 256], here)

        def corner_rolls(n):
            roll_all(n, ((0, 0, 3), (1, 1, 3), (2, 2, -3), (3, 3, -3), (4, 0, 1), (5, 1, -1), (8, 2, 1), (9, 3, -1)))

        def middle_rows(n):
            for tile in range(tiles):
                upper = (lane + tile * 128) % 9 < 3
                for b in range(2):
                    gram[rows_of(4 + b, n), place(tile)] = gram[rows_of(4 + b, n), place(tile)] + jnp.where(
                        upper, from_right(n, 2 + b, tile, 3), from_left(n, b, tile, 3)
                    )

        def middle_rolls(n):
            roll_all(n, ((6, 4, 1), (7, 5, -1)))

        def write(n):
            for tile in range(tiles):
                first = (lane + tile * 128) % 3 == 0
                for a, left in enumerate((0, 4, 2)):
                    middle = gram[rows_of(6 + a, n), place(tile)] + jnp.where(
                        first, from_right(n, 5 + 2 * a, tile, 1), from_left(n, 4 + 2 * a, tile, 1)
                    )
                    taps = (gram[rows_of(left, n), place(tile)], middle, gram[rows_of(left + 1, n), place(tile)])
                    for b in range(3):
                        spread[tile % 4, pl.ds(3 * a + b, 8, stride=9), :] = taps[b]
                end = min(columns, tile * 128 + 128)
                cut = slice(tile * 128, end)
                rows = slice(n * 72, n * 72 + 72)
                out_ref[rows, cut] = (
                    decay_rate * covariance_ref[rows, cut]
                    + new_share * spread[tile % 4][:, : end - tile * 128]
                )

        slabs = sub // 8
        corner_rolls(0)
        for n in range(slabs):
            middle_rows(n)
            middle_rolls(n)
            if n + 1 < slabs:
                corner_rolls(n + 1)
            write(n)

    pair = (even, odd)

    @pl.when(i == 0)
    def _():
        multiply(pair[0])

    for parity in range(2):

        @pl.when((i > 0) & (i < groups) & (i % 2 == parity))
        def _(parity=parity):
            multiply(pair[parity])
            finish(pair[1 - parity])

    @pl.when(i == groups)
    def _():
        finish(pair[(groups - 1) % 2])


def combine(row, patches, low, side, sel, covariance, width, height):
    repeats, wide, batch, channels, lanes = row.shape
    positions = wide * batch * lanes
    columns = covariance.shape[1]
    unit = 8 * parts
    group = max(g for g in range(unit, 121, unit) if channels % g == 0)
    groups = repeats * channels // group
    padded = low.shape[0]
    once = pl.Buffered(1)

    def resident(array):
        return pl.BlockSpec(array.shape, lambda t: (0,) * array.ndim, pipeline_mode=once)

    anywhere = pl.BlockSpec(memory_space=pl.ANY)
    tile = pl.BlockSpec((group // parts * 9, columns), lambda t: (jnp.maximum(t - parts, 0), 0))
    return pl.pallas_call(
        functools.partial(combine_kernel, width, height, (1.0 - decay_rate) / positions),
        grid=((groups + 1) * parts,),
        out_shape=jax.ShapeDtypeStruct(covariance.shape, jnp.float32),
        in_specs=[resident(row), resident(low), resident(side), anywhere, anywhere, tile],
        out_specs=tile,
        scratch_shapes=[
            pltpu.VMEM((padded, positions), jnp.bfloat16),
            pltpu.VMEM((repeats, channels, sel.shape[0]), jnp.float32),
            pltpu.VMEM((4 * group, positions), jnp.bfloat16),
            pltpu.VMEM((2 * group, low.shape[1]), jnp.bfloat16),
            pltpu.VMEM((3 * group, side.shape[1]), jnp.bfloat16),
            pltpu.VMEM((9 * group, 128 + padded), jnp.float32),
            pltpu.VMEM((9 * group, 128 + padded), jnp.float32),
            pltpu.VMEM((2, 10, 8, -(-columns // 128) * 128), jnp.float32),
            pltpu.VMEM((4, 72, 128), jnp.float32),
            pltpu.SemaphoreType.DMA((parts + 1,)),
        ],
        cost_estimate=pl.CostEstimate(
            flops=2 * 4 * repeats * channels * positions * columns,
            bytes_accessed=covariance.size * 8 + patches.size * 2,
            transcendentals=0,
        ),
        compiler_params=pltpu.CompilerParams(vmem_limit_bytes=67043328),
    )(row, low, side, sel, patches, covariance)


def shards(activations, covariance):
    wide = lax.axis_size("wide")
    narrow = lax.axis_size("narrow")
    batch, rows, width, channels = activations.shape
    height = rows * wide
    lanes = rows * width
    if lanes % 128 or channels % 16 or wide % 2 or narrow % wide or width != height:
        return plain(activations, covariance)
    own = jnp.transpose(activations.reshape(batch, lanes, channels), (0, 2, 1))
    row, patches, low, side, sel = gather(own, wide, narrow, width, height)
    return combine(row, patches, low, side, sel, covariance, width, height)


def solution(mesh):
    return jax.shard_map(
        shards,
        mesh=mesh,
        in_specs=(P(None, "wide", None, "narrow"), P("wide", "narrow")),
        out_specs=P("wide", "narrow"),
        check_vma=False,
    )
```

```python
import functools

import jax
import jax.numpy as jnp
from jax import lax
from jax.experimental import pallas as pl
from jax.experimental.pallas import tpu as pltpu
from jax.sharding import PartitionSpec as P

decay_rate = 0.9


def expand_kernel(width, height, image_ref, out_ref, spread):
    group, positions = image_ref.shape
    image = image_ref[...].astype(jnp.float32)
    place = lax.broadcasted_iota(jnp.int32, (8, positions), 1)
    column = place % width
    row = (place // width) % height
    row_ok = [row >= 1, None, row < height - 1]
    column_ok = [column >= 1, None, column < width - 1]
    for a in range(3):
        for b in range(3):
            offset = (a - 1) * width + (b - 1)
            moved = pltpu.roll(image, (-offset) % positions, 1) if offset else image
            keep = row_ok[a]
            if column_ok[b] is not None:
                keep = column_ok[b] if keep is None else keep & column_ok[b]
            for half in range(group // 8):
                part = moved[half * 8 : half * 8 + 8]
                if keep is not None:
                    part = jnp.where(keep, part, 0.0)
                for tile in range(positions // 128):
                    spread[tile, pl.ds(half * 72 + 3 * a + b, 8, stride=9), :] = part[
                        :, tile * 128 : tile * 128 + 128
                    ]
    for tile in range(positions // 128):
        out_ref[:, tile * 128 : tile * 128 + 128] = spread[tile].astype(jnp.bfloat16)


def expand(image, width, height):
    channels, positions = image.shape
    group = 16 if channels % 16 == 0 else 8
    return pl.pallas_call(
        functools.partial(expand_kernel, width, height),
        grid=(channels // group,),
        out_shape=jax.ShapeDtypeStruct((channels * 9, positions), jnp.bfloat16),
        in_specs=[pl.BlockSpec((group, positions), lambda i: (i, 0))],
        out_specs=pl.BlockSpec((group * 9, positions), lambda i: (i, 0)),
        scratch_shapes=[pltpu.VMEM((positions // 128, group * 9, 128), jnp.float32)],
        cost_estimate=pl.CostEstimate(
            flops=channels * 9 * positions * 20,
            bytes_accessed=channels * positions * 20,
            transcendentals=0,
        ),
    )(image)


def update_kernel(width, height, new_share, image_ref, edge_ref, patches_ref, low_ref, side_ref, covariance_ref, *rest):
    out_ref, corners, gram, spread = rest[-4:]
    group, positions = image_ref.shape
    columns = covariance_ref.shape[1]
    tiles = -(-columns // 128)
    image = image_ref[...].astype(jnp.float32)
    place = lax.broadcasted_iota(jnp.int32, (1, positions), 1)
    column = place % width
    row = (place // width) % height
    row_ok = [row >= 1, None, row < height - 1]
    column_ok = [column >= 1, None, column < width - 1]
    planes = []
    for a, b in ((0, 0), (0, 2), (2, 0), (2, 2)):
        offset = (a - 1) * width + (b - 1)
        moved = pltpu.roll(image, (-offset) % positions, 1)
        planes.append(jnp.where(row_ok[a] & column_ok[b], moved, 0.0))
    corners[...] = jnp.concatenate(planes, axis=0).astype(jnp.bfloat16)
    contract = (((1,), (1,)), ((), ()))
    gram[0 : 4 * group, 128 : 128 + columns] = lax.dot_general(
        corners[...], patches_ref[...], contract, preferred_element_type=jnp.float32
    )
    size = low_ref.shape[1]
    edge = edge_ref[...].astype(jnp.float32)
    edge = [edge[:, k * size : k * size + size] for k in (0, 2, 3, 4, 5)]
    low = lax.dot_general(
        jnp.concatenate(edge[:2], axis=0).astype(jnp.bfloat16), low_ref[...], contract, preferred_element_type=jnp.float32
    )
    gram[4 * group : 6 * group, 128 : 128 + columns] = low
    side = lax.dot_general(
        jnp.concatenate(edge[2:], axis=0).astype(jnp.bfloat16), side_ref[...], contract, preferred_element_type=jnp.float32
    )
    gram[6 * group : 9 * group, 128 : 128 + columns] = side

    def shifted(plane, tile, by):
        near = gram[plane * group : plane * group + group, tile * 128 : tile * 128 + 384]
        return pltpu.roll(near, by % 384, 1)[:, 128:256]

    for tile in range(tiles):
        tap = (lax.broadcasted_iota(jnp.int32, (1, 128), 1) + tile * 128) % 9
        here = slice(128 + tile * 128, 256 + tile * 128)
        for b in range(2):
            mine = slice((4 + b) * group, (5 + b) * group)
            gram[mine, here] = gram[mine, here] + jnp.where(
                tap < 3, shifted(2 + b, tile, -3), shifted(b, tile, 3)
            )
    first = (0, 4, 2)
    for tile in range(tiles):
        lane = lax.broadcasted_iota(jnp.int32, (1, 128), 1) + tile * 128
        here = slice(128 + tile * 128, 256 + tile * 128)
        for a in range(3):
            left = first[a]
            middle = gram[(6 + a) * group : (7 + a) * group, here] + jnp.where(
                lane % 3 == 0, shifted(left + 1, tile, -1), shifted(left, tile, 1)
            )
            taps = (
                gram[left * group : (left + 1) * group, here],
                middle,
                gram[(left + 1) * group : (left + 2) * group, here],
            )
            for b in range(3):
                spread[tile, pl.ds(3 * a + b, group, stride=9), :] = taps[b]
        end = min(columns, tile * 128 + 128)
        cut = slice(tile * 128, end)
        out_ref[:, cut] = (
            decay_rate * covariance_ref[:, cut] + new_share * spread[tile][:, : end - tile * 128]
        )


def update(image, edges, patches, low, side, covariance, group, first, steps, slabs, so_far, width, height):
    channels, positions = image.shape
    columns = covariance.shape[1]
    each = covariance.shape[0] // (9 * group * slabs)
    padded = -(-columns // 128) * 128 + 256
    whole = lambda i: (0, 0)
    once = pl.Buffered(1)
    tile = pl.BlockSpec(
        (group * 9, columns), lambda i: ((i // steps) * each + first + i % steps, 0)
    )
    operands = [image, edges, patches, low, side, covariance]
    specs = [
        pl.BlockSpec((group, positions), lambda i: (i, 0)),
        pl.BlockSpec((group, edges.shape[1]), lambda i: (i, 0)),
        pl.BlockSpec(patches.shape, whole, pipeline_mode=once),
        pl.BlockSpec(low.shape, whole, pipeline_mode=once),
        pl.BlockSpec(side.shape, whole, pipeline_mode=once),
        tile,
    ]
    aliases = {}
    if so_far is not None:
        operands.append(so_far)
        specs.append(pl.BlockSpec(memory_space=pl.ANY))
        aliases = {6: 0}
    return pl.pallas_call(
        functools.partial(update_kernel, width, height, (1.0 - decay_rate) / positions),
        grid=(slabs * steps,),
        out_shape=jax.ShapeDtypeStruct(covariance.shape, jnp.float32),
        in_specs=specs,
        out_specs=tile,
        scratch_shapes=[
            pltpu.VMEM((4 * group, positions), jnp.bfloat16),
            pltpu.VMEM((9 * group, padded), jnp.float32),
            pltpu.VMEM((-(-columns // 128), group * 9, 128), jnp.float32),
        ],
        input_output_aliases=aliases,
        cost_estimate=pl.CostEstimate(
            flops=2 * 4 * channels * positions * columns,
            bytes_accessed=channels * 9 * columns * 8 + patches.size * 2,
            transcendentals=0,
        ),
        compiler_params=pltpu.CompilerParams(vmem_limit_bytes=62 * 1024 * 1024),
    )(*operands)


def edge_selector(batch, height, width):
    place = lax.broadcasted_iota(jnp.int32, (batch * height * width, 1), 0)
    parts = []
    for size, last, stride in ((width, (height - 1) * width, 1), (height, width - 1, width)):
        line = lax.broadcasted_iota(jnp.int32, (1, batch * size), 1)
        for k in (-1, 0, 1):
            at = line % size + k
            wanted = (line // size) * height * width + last + at * stride
            parts.append((place == wanted) & (at >= 0) & (at < size))
    return jnp.concatenate(parts, axis=1).astype(jnp.bfloat16)


def edge_values(image, selector):
    return lax.dot_general(
        image, selector, (((1,), (0,)), ((), ())), preferred_element_type=jnp.float32
    ).astype(jnp.bfloat16)


def interleave(planes):
    empty = jnp.zeros_like(next(iter(planes.values())))
    stacked = jnp.stack([planes.get(t, empty) for t in range(9)], axis=1)
    return stacked.reshape(-1, stacked.shape[2])


def plain(activations, covariance):
    wide_count = lax.axis_size("wide")
    narrow_count = lax.axis_size("narrow")
    repeats = narrow_count // wide_count
    batch, rows, width, channels = activations.shape
    height = rows * wide_count
    strip = jnp.transpose(activations.reshape(batch * rows * width, channels)).reshape(
        channels, batch, rows * width
    )
    moves = []
    for r in range(wide_count):
        for s in range(narrow_count):
            target = (s // repeats) * narrow_count + r + (s % repeats) * wide_count
            moves.append((r * narrow_count + s, target))
    row_strip = lax.ppermute(strip, ("wide", "narrow"), moves)
    group = max(g for g in range(8, 49, 8) if channels % g == 0)
    steps = channels // group
    cuts = [0, (steps * 2) // 5, steps] if steps > 3 else [0, steps]
    positions = batch * height * width
    column_strips = lax.all_gather(strip, "wide")
    row_parts = []
    for low_cut, high_cut in zip(cuts[:-1], cuts[1:]):
        piece = row_strip[low_cut * group : high_cut * group]
        if row_parts:
            piece, row_parts[-1] = lax.optimization_barrier((piece, row_parts[-1]))
        row_parts.append(lax.all_gather(piece, "narrow"))
    selector = edge_selector(batch, height, width)
    column_image = jnp.transpose(column_strips, (1, 2, 0, 3)).reshape(channels, positions)
    patches = expand(column_image, width, height)
    edges = edge_values(column_image, selector)
    size = edges.shape[1] // 6
    edge = [edges[:, k * size : k * size + size] for k in range(6)]
    low = interleave({3 + b: edge[b] for b in range(3)})
    side = interleave({3 * a + 1: edge[3 + a] for a in range(3)})
    updated = None
    for part, first in enumerate(cuts[:-1]):
        count = cuts[part + 1] - first
        own = count * group
        image = jnp.transpose(
            row_parts[part].reshape(repeats, wide_count, own, batch, rows * width), (0, 2, 3, 1, 4)
        ).reshape(repeats * own, positions)
        edges = edge_values(image, selector)
        updated = update(
            image, edges, patches, low, side, covariance, group, first, count, repeats, updated, width, height
        )
    return updated


MESH = pl.DeviceIdType.MESH


def expand_group(channels):
    return max(g for g in (16, 32, 48) if channels % g == 0)


def roll_taps(image, width, height):
    positions = image.shape[1]
    place = lax.broadcasted_iota(jnp.int32, (8, positions), 1)
    column = place % width
    row = (place // width) % height
    return [row >= 1, None, row < height - 1], [column >= 1, None, column < width - 1]


def gather_kernel(shape, own_ref, row_ref, patches_ref, low_ref, side_ref, sel_ref, *rest):
    (
        col, spread, staged, sel, edges, line,
        own_send, own_recv, pass_send, row_send, row_recv, local, out_sem,
    ) = rest
    width, height, wide, narrow, inner = shape
    repeats, _, batch, channels, lanes = row_ref.shape
    outer = narrow // inner
    pairs = wide // 2
    r = lax.axis_index("wide")
    s = lax.axis_index("narrow")
    z, y = s // inner, s % inner
    pair, core = r // 2, r % 2
    sibling = pair * 2 + 1 - core
    others = [((pair + p) % pairs) * 2 + core for p in range(1, pairs)]
    steps = ((z + 1 < outer, z + 1, y), (z > 0, z - 1, y), (y + 1 < inner, z, y + 1), (y > 0, z, y - 1))

    barrier = pltpu.get_barrier_semaphore()
    for q in [sibling] + others:
        pl.semaphore_signal(barrier, inc=1, device_id=(q, s), device_id_type=MESH)
    for there, to_z, to_y in steps:

        @pl.when(there)
        def _(to_z=to_z, to_y=to_y):
            pl.semaphore_signal(barrier, inc=1, device_id=(r, to_z * inner + to_y), device_id_type=MESH)

    greeted = pairs
    for there, _, _ in steps:
        greeted = greeted + jnp.where(there, 1, 0)
    pl.semaphore_wait(barrier, greeted)

    def to_core(source, strip, b, q, send):
        return pltpu.make_async_remote_copy(
            src_ref=source,
            dst_ref=col.at[strip, b],
            send_sem=send,
            recv_sem=own_recv.at[strip, b],
            device_id=(q, s),
            device_id_type=MESH,
        )

    def first_sends(b):
        return [to_core(own_ref.at[b], r, b, q, own_send.at[n, b]) for n, q in enumerate([sibling] + others)]

    for b in range(batch):
        for copy in first_sends(b):
            copy.start()
    mine = pltpu.make_async_copy(own_ref, col.at[r], local.at[repeats])
    mine.start()

    order = [r, sibling]
    for q in others:
        order += [q, (q // 2) * 2 + 1 - core]

    streams = []
    for k in range(repeats):
        source = r * repeats + k
        from_z, from_y = source // inner, source % inner
        on = y == from_y
        children = (
            (steps[0][0] & on & (z >= from_z), steps[0]),
            (steps[1][0] & on & (z <= from_z), steps[1]),
            (steps[2][0] & (y >= from_y), steps[2]),
            (steps[3][0] & (y <= from_y), steps[3]),
        )
        any_child = children[0][0] | children[1][0] | children[2][0] | children[3][0]
        streams.append((s == source, any_child, children))

    cut = -(-channels // 32) * 16
    halves = (pl.ds(0, cut), pl.ds(cut, channels - cut))

    def onward(k, j, b, h, source):
        for n, (there, (_, to_z, to_y)) in enumerate(streams[k][2]):

            @pl.when(there)
            def _(n=n, to_z=to_z, to_y=to_y):
                pltpu.make_async_remote_copy(
                    src_ref=source.at[halves[h]],
                    dst_ref=row_ref.at[k, order[j], b, halves[h]],
                    send_sem=row_send.at[k, n],
                    recv_sem=row_recv.at[k, j, b, h],
                    device_id=(r, to_z * inner + to_y),
                    device_id_type=MESH,
                ).start()

    def landed(k, j, b, h):
        ref = row_ref.at[k, order[j], b, halves[h]]
        pltpu.make_async_copy(ref, ref, row_recv.at[k, j, b, h]).wait()

    def passed(p, b):
        strip = order[2 * p]
        return to_core(col.at[strip, b], strip, b, sibling, pass_send.at[p - 1, b])

    group = expand_group(channels)
    rows = group * 9
    expansions = channels // group
    share = -(-expansions // (2 * wide))
    block = height * width
    positions = batch * block
    lines = batch * height
    line[...] = jnp.zeros_like(line)
    for ref in (low_ref, side_ref):
        ref[channels * 9 :, :] = jnp.zeros((ref.shape[0] - channels * 9, ref.shape[1]), jnp.bfloat16)

    def written(e, b, slot):
        top = pl.multiple_of(e * rows, 16)
        left = pl.multiple_of(b * block, 128)
        return pltpu.make_async_copy(
            staged.at[slot], patches_ref.at[pl.ds(top, rows), pl.ds(left, block)], out_sem.at[slot]
        )

    def expand_step(e, b):
        turn = b * expansions + e
        slot = turn % 2

        @pl.when(turn >= 2)
        def _():
            written(0, 0, slot).wait()

        first = pl.multiple_of(e * group, 16)
        image = jnp.concatenate([col[w, b, pl.ds(first, group), :] for w in range(wide)], axis=1).astype(jnp.float32)
        row_ok, column_ok = roll_taps(image, width, height)
        for a in range(3):
            for c in range(3):
                offset = (a - 1) * width + (c - 1)
                moved = pltpu.roll(image, (-offset) % block, 1) if offset else image
                keep = row_ok[a]
                if column_ok[c] is not None:
                    keep = column_ok[c] if keep is None else keep & column_ok[c]
                for half in range(group // 8):
                    part = moved[half * 8 : half * 8 + 8]
                    if keep is not None:
                        part = jnp.where(keep, part, 0.0)
                    for tile in range(block // 128):
                        spread[tile, pl.ds(half * 72 + 3 * a + c, 8, stride=9), :] = part[
                            :, tile * 128 : tile * 128 + 128
                        ]
        for tile in range(block // 128):
            staged[slot, :, tile * 128 : tile * 128 + 128] = spread[tile].astype(jnp.bfloat16)
        written(e, b, slot).start()

    mine.wait()
    sel_copy = pltpu.make_async_copy(sel, sel_ref, local.at[repeats + 1])

    def select():
        at = lax.broadcasted_iota(jnp.int32, (1, positions), 1)
        across = lax.broadcasted_iota(jnp.int32, (batch * width, 1), 0)
        down = lax.broadcasted_iota(jnp.int32, (lines, 1), 0)
        low_at = (across // width) * block + (height - 1) * width + across % width
        side_at = (down // height) * block + (down % height) * width + width - 1
        for n, wanted in enumerate((low_at, side_at)):
            sel[n * batch * width : n * batch * width + wanted.shape[0], :] = (
                (at == wanted).astype(jnp.float32).astype(jnp.bfloat16)
            )
        sel_copy.start()

    def turn(b, _):
        for j in range(wide):
            if j > 0:
                to_core(col.at[order[j], b], order[j], b, sibling, own_send.at[0, b]).wait_recv()
            if j > 1 and j % 2 == 0:
                passed(j // 2, b).start()
            for k in range(repeats):

                @pl.when(streams[k][0])
                def _(k=k):
                    for h in range(2):
                        onward(k, j, b, h, col.at[order[j], b])

        pl.when(b == 0)(select)
        for j in range(wide):
            for h in range(2):
                for k in range(repeats):

                    @pl.when(jnp.logical_not(streams[k][0]) & streams[k][1])
                    def _(k=k, h=h):
                        landed(k, j, b, h)
                        onward(k, j, b, h, row_ref.at[k, order[j], b])

                slot = 2 * j + h
                lax.fori_loop(
                    min(expansions, slot * share),
                    min(expansions, slot * share + share),
                    lambda e, _: (expand_step(e, b), 0)[1],
                    0,
                )

        return 0

    lax.fori_loop(0, batch, turn, 0)
    for k in range(repeats):

        @pl.when(streams[k][0])
        def _(k=k):
            pltpu.make_async_copy(col, row_ref.at[k], local.at[k]).start()

    pieces = [col[w, n] for n in range(batch) for w in range(wide)]
    edges[...] = lax.dot_general(
        jnp.concatenate(pieces, axis=1), sel[...], (((1,), (1,)), ((), ())), preferred_element_type=jnp.float32
    )

    def edge_step(e, _):
        first = pl.multiple_of(e * 16, 16)
        edge = edges[pl.ds(first, 16), :]
        for n, (size, base, stride) in enumerate(((width, 3, 1), (height, 1, 3))):
            count = batch * size
            value = edge[:, n * batch * width : n * batch * width + count]
            spot = lax.broadcasted_iota(jnp.int32, (16, count), 1) % size
            for k in (-1, 0, 1):
                moved = pltpu.roll(value, (-k) % count, 1) if k else value
                moved = jnp.where((spot + k >= 0) & (spot + k < size), moved, 0.0)
                for half in range(16 // 8):
                    line[n, pl.ds(half * 72 + base + (k + 1) * stride, 8, stride=9), :] = moved[
                        half * 8 : half * 8 + 8
                    ]
        top = pl.multiple_of(e * 144, 16)
        low_ref[pl.ds(top, 144), :] = line[0].astype(jnp.bfloat16)
        side_ref[pl.ds(top, 144), :] = line[1].astype(jnp.bfloat16)
        return 0

    lax.fori_loop(0, channels // 16, edge_step, 0)
    for k in range(repeats):

        @pl.when(jnp.logical_not(streams[k][0]) & jnp.logical_not(streams[k][1]))
        def _(k=k):
            for b in range(batch):
                for j in range(wide):
                    for h in range(2):
                        landed(k, j, b, h)

    for slot in range(min(2, batch * expansions)):
        written(0, 0, slot).wait()
    sel_copy.wait()
    for b in range(batch):
        for copy in first_sends(b):
            copy.wait_send()
        for p in range(1, pairs):
            passed(p, b).wait_send()
    for k in range(repeats):
        for n, (there, _) in enumerate(streams[k][2]):

            @pl.when(there)
            def _(k=k, n=n):
                pltpu.make_async_copy(row_ref.at[k], row_ref.at[k], row_send.at[k, n]).wait()

        @pl.when(streams[k][0])
        def _(k=k):
            pltpu.make_async_copy(col, row_ref.at[k], local.at[k]).wait()


def gather(own, wide, narrow, width, height):
    batch, channels, lanes = own.shape
    repeats = narrow // wide
    inner = max(d for d in range(1, narrow + 1) if narrow % d == 0 and d * d <= narrow)
    positions = batch * wide * lanes
    lines = batch * (width + height)
    padded = padded_columns(channels * 9)
    anywhere = pl.BlockSpec(memory_space=pl.ANY)
    vmem = pl.BlockSpec(memory_space=pltpu.VMEM)
    bf16 = jnp.bfloat16
    return pl.pallas_call(
        functools.partial(gather_kernel, (width, height, wide, narrow, inner)),
        out_shape=[
            jax.ShapeDtypeStruct((repeats, wide, batch, channels, lanes), bf16),
            jax.ShapeDtypeStruct((channels * 9, positions), bf16),
            jax.ShapeDtypeStruct((padded, batch * width), bf16),
            jax.ShapeDtypeStruct((padded, batch * height), bf16),
            jax.ShapeDtypeStruct((lines, positions), bf16),
        ],
        in_specs=[vmem],
        out_specs=[anywhere, anywhere, vmem, vmem, anywhere],
        scratch_shapes=[
            pltpu.VMEM((wide, batch, channels, lanes), bf16),
            pltpu.VMEM((wide * lanes // 128, expand_group(channels) * 9, 128), jnp.float32),
            pltpu.VMEM((2, expand_group(channels) * 9, wide * lanes), bf16),
            pltpu.VMEM((lines, positions), bf16),
            pltpu.VMEM((channels, lines), jnp.float32),
            pltpu.VMEM((2, 144, batch * width), jnp.float32),
            pltpu.SemaphoreType.DMA((wide // 2, batch)),
            pltpu.SemaphoreType.DMA((wide, batch)),
            pltpu.SemaphoreType.DMA((max(1, wide // 2 - 1), batch)),
            pltpu.SemaphoreType.DMA((repeats, 4)),
            pltpu.SemaphoreType.DMA((repeats, wide, batch, 2)),
            pltpu.SemaphoreType.DMA((repeats + 2,)),
            pltpu.SemaphoreType.DMA((2,)),
        ],
        compiler_params=pltpu.CompilerParams(
            collective_id=0, has_side_effects=True, vmem_limit_bytes=60 * 1024 * 1024
        ),
    )(own)


parts = 3


def padded_columns(columns):
    return -(-columns // (256 * parts)) * 256 * parts


def combine_kernel(
    width, height, new_share, row_ref, low_ref, side_ref, sel_ref, patches_ref, covariance_ref, out_ref,
    patches, edges, corners, low_rows, side_rows, even, odd, rolled, spread, fetched,
):
    repeats, wide, batch, channels, lanes = row_ref.shape
    positions = wide * batch * lanes
    group = corners.shape[0] // 4
    steps = channels // group
    groups = repeats * steps
    sub = group // parts
    columns = covariance_ref.shape[1]
    tiles = -(-columns // 128)
    chunk = patches.shape[0] // parts
    at = pl.program_id(0)
    i, j = at // parts, at % parts
    size = low_ref.shape[1]
    lines = sel_ref.shape[0]
    contract = (((1,), (1,)), ((), ()))

    pieces = [n for n in range(parts) if n * chunk < columns]

    def fetch(n):
        rows = pl.ds(n * chunk, min(chunk, columns - n * chunk))
        return pltpu.make_async_copy(patches_ref.at[rows, :], patches.at[rows, :], fetched.at[n])

    selector = pltpu.make_async_copy(sel_ref, corners.at[pl.ds(0, lines), :], fetched.at[parts])

    @pl.when(at == 0)
    def _():
        selector.start()
        for n in pieces:
            fetch(n).start()
        patches[columns:, :] = jnp.zeros((patches.shape[0] - columns, positions), jnp.bfloat16)
        selector.wait()
        for k in range(repeats):
            whole = jnp.concatenate([row_ref[k, w, n] for n in range(batch) for w in range(wide)], axis=1)
            edges[k] = lax.dot_general(whole, corners[0:lines, :], contract, preferred_element_type=jnp.float32)

    def edge_taps(value, length, taps):
        count = value.shape[1]
        spot = lax.broadcasted_iota(jnp.int32, value.shape, 1) % length
        out = []
        for by in taps:
            moved = pltpu.roll(value, (-by) % count, 1) if by else value
            out.append(jnp.where((spot + by >= 0) & (spot + by < length), moved, 0.0))
        return jnp.concatenate(out, axis=0).astype(jnp.bfloat16)

    @pl.when((j == 0) & (i < groups))
    def _():
        k = i // steps
        first = pl.multiple_of((i % steps) * group, 8)
        image = jnp.concatenate(
            [row_ref[k, w, n, pl.ds(first, group), :] for n in range(batch) for w in range(wide)], axis=1
        ).astype(jnp.float32)
        place = lax.broadcasted_iota(jnp.int32, (1, positions), 1)
        column = place % width
        row = (place // width) % height
        row_ok = [row >= 1, None, row < height - 1]
        column_ok = [column >= 1, None, column < width - 1]
        for n, (a, b) in enumerate(((0, 0), (0, 2), (2, 0), (2, 2))):
            offset = (a - 1) * width + (b - 1)
            moved = pltpu.roll(image, (-offset) % positions, 1)
            moved = jnp.where(row_ok[a] & column_ok[b], moved, 0.0)
            corners[n * group : n * group + group, :] = moved.astype(jnp.bfloat16)
        edge = edges[k, pl.ds(first, group), :]
        low_rows[...] = edge_taps(edge[:, :size], width, (-1, 1))
        side_rows[...] = edge_taps(edge[:, size:], height, (-1, 0, 1))

    for n in pieces:

        @pl.when(at == n)
        def _(n=n):
            fetch(n).wait()

    def multiply(gram):
        for piece in range(chunk // 256):
            start = pl.multiple_of(j * chunk + piece * 256, 256)
            here = pl.ds(pl.multiple_of(128 + start, 128), 256)
            rows = pl.ds(start, 256)
            for left, right, top, count in (
                (corners, patches, 0, 4),
                (low_rows, low_ref, 4, 2),
                (side_rows, side_ref, 6, 3),
            ):
                gram[top * group : (top + count) * group, here] = lax.dot_general(
                    left[...], right[rows, :], contract, preferred_element_type=jnp.float32
                )

    lane = lax.broadcasted_iota(jnp.int32, (8, 128), 1)

    def finish(gram):
        def rows_of(p, n):
            return pl.ds(pl.multiple_of(p * group + j * sub + n * 8, 8), 8)

        def place(tile):
            return slice(128 + tile * 128, 256 + tile * 128)

        def roll_all(n, wanted):
            for q, p, by in wanted:
                rolled[n % 2, q] = pltpu.roll(gram[rows_of(p, n), 128 : 128 + tiles * 128], by % (tiles * 128), 1)

        def moved(n, q, tile):
            return rolled[n % 2, q, :, tile * 128 : tile * 128 + 128]

        def corner_rolls(n):
            roll_all(n, ((0, 0, 3), (1, 1, 3), (2, 2, -3), (3, 3, -3), (4, 0, 1), (5, 1, -1), (8, 2, 1), (9, 3, -1)))

        def middle_rows(n):
            for tile in range(tiles):
                upper = (lane + tile * 128) % 9 < 3
                for b in range(2):
                    gram[rows_of(4 + b, n), place(tile)] = gram[rows_of(4 + b, n), place(tile)] + jnp.where(
                        upper, moved(n, 2 + b, tile), moved(n, b, tile)
                    )

        def middle_rolls(n):
            roll_all(n, ((6, 4, 1), (7, 5, -1)))

        def write(n):
            for tile in range(tiles):
                first = (lane + tile * 128) % 3 == 0
                for a, left in enumerate((0, 4, 2)):
                    middle = gram[rows_of(6 + a, n), place(tile)] + jnp.where(
                        first, moved(n, 5 + 2 * a, tile), moved(n, 4 + 2 * a, tile)
                    )
                    taps = (gram[rows_of(left, n), place(tile)], middle, gram[rows_of(left + 1, n), place(tile)])
                    for b in range(3):
                        spread[tile % 4, pl.ds(3 * a + b, 8, stride=9), :] = taps[b]
                end = min(columns, tile * 128 + 128)
                cut = slice(tile * 128, end)
                rows = slice(n * 72, n * 72 + 72)
                out_ref[rows, cut] = (
                    decay_rate * covariance_ref[rows, cut]
                    + new_share * spread[tile % 4][:, : end - tile * 128]
                )

        slabs = sub // 8
        corner_rolls(0)
        for n in range(slabs):
            middle_rows(n)
            middle_rolls(n)
            if n + 1 < slabs:
                corner_rolls(n + 1)
            write(n)

    pair = (even, odd)

    @pl.when(i == 0)
    def _():
        multiply(pair[0])

    for parity in range(2):

        @pl.when((i > 0) & (i < groups) & (i % 2 == parity))
        def _(parity=parity):
            multiply(pair[parity])
            finish(pair[1 - parity])

    @pl.when(i == groups)
    def _():
        finish(pair[(groups - 1) % 2])


def combine(row, patches, low, side, sel, covariance, width, height):
    repeats, wide, batch, channels, lanes = row.shape
    positions = wide * batch * lanes
    columns = covariance.shape[1]
    unit = 8 * parts
    group = max(g for g in range(unit, 121, unit) if channels % g == 0)
    groups = repeats * channels // group
    padded = low.shape[0]
    once = pl.Buffered(1)

    def resident(array):
        return pl.BlockSpec(array.shape, lambda t: (0,) * array.ndim, pipeline_mode=once)

    anywhere = pl.BlockSpec(memory_space=pl.ANY)
    tile = pl.BlockSpec((group // parts * 9, columns), lambda t: (jnp.maximum(t - parts, 0), 0))
    return pl.pallas_call(
        functools.partial(combine_kernel, width, height, (1.0 - decay_rate) / positions),
        grid=((groups + 1) * parts,),
        out_shape=jax.ShapeDtypeStruct(covariance.shape, jnp.float32),
        in_specs=[resident(row), resident(low), resident(side), anywhere, anywhere, tile],
        out_specs=tile,
        scratch_shapes=[
            pltpu.VMEM((padded, positions), jnp.bfloat16),
            pltpu.VMEM((repeats, channels, sel.shape[0]), jnp.float32),
            pltpu.VMEM((4 * group, positions), jnp.bfloat16),
            pltpu.VMEM((2 * group, low.shape[1]), jnp.bfloat16),
            pltpu.VMEM((3 * group, side.shape[1]), jnp.bfloat16),
            pltpu.VMEM((9 * group, 128 + padded), jnp.float32),
            pltpu.VMEM((9 * group, 128 + padded), jnp.float32),
            pltpu.VMEM((2, 10, 8, -(-columns // 128) * 128), jnp.float32),
            pltpu.VMEM((4, 72, 128), jnp.float32),
            pltpu.SemaphoreType.DMA((parts + 1,)),
        ],
        cost_estimate=pl.CostEstimate(
            flops=2 * 4 * repeats * channels * positions * columns,
            bytes_accessed=covariance.size * 8 + patches.size * 2,
            transcendentals=0,
        ),
        compiler_params=pltpu.CompilerParams(vmem_limit_bytes=67043328),
    )(row, low, side, sel, patches, covariance)


def shards(activations, covariance):
    wide = lax.axis_size("wide")
    narrow = lax.axis_size("narrow")
    batch, rows, width, channels = activations.shape
    height = rows * wide
    lanes = rows * width
    if lanes % 128 or channels % 16 or wide % 2 or narrow % wide or width != height:
        return plain(activations, covariance)
    own = jnp.transpose(activations.reshape(batch, lanes, channels), (0, 2, 1))
    row, patches, low, side, sel = gather(own, wide, narrow, width, height)
    return combine(row, patches, low, side, sel, covariance, width, height)


def solution(mesh):
    return jax.shard_map(
        shards,
        mesh=mesh,
        in_specs=(P(None, "wide", None, "narrow"), P("wide", "narrow")),
        out_specs=P("wide", "narrow"),
        check_vma=False,
    )
```

```python
import functools

import jax
import jax.numpy as jnp
from jax import lax
from jax.experimental import pallas as pl
from jax.experimental.pallas import tpu as pltpu
from jax.sharding import PartitionSpec as P

decay_rate = 0.9


def expand_kernel(width, height, image_ref, out_ref, spread):
    group, positions = image_ref.shape
    image = image_ref[...].astype(jnp.float32)
    place = lax.broadcasted_iota(jnp.int32, (8, positions), 1)
    column = place % width
    row = (place // width) % height
    row_ok = [row >= 1, None, row < height - 1]
    column_ok = [column >= 1, None, column < width - 1]
    for a in range(3):
        for b in range(3):
            offset = (a - 1) * width + (b - 1)
            moved = pltpu.roll(image, (-offset) % positions, 1) if offset else image
            keep = row_ok[a]
            if column_ok[b] is not None:
                keep = column_ok[b] if keep is None else keep & column_ok[b]
            for half in range(group // 8):
                part = moved[half * 8 : half * 8 + 8]
                if keep is not None:
                    part = jnp.where(keep, part, 0.0)
                for tile in range(positions // 128):
                    spread[tile, pl.ds(half * 72 + 3 * a + b, 8, stride=9), :] = part[
                        :, tile * 128 : tile * 128 + 128
                    ]
    for tile in range(positions // 128):
        out_ref[:, tile * 128 : tile * 128 + 128] = spread[tile].astype(jnp.bfloat16)


def expand(image, width, height):
    channels, positions = image.shape
    group = 16 if channels % 16 == 0 else 8
    return pl.pallas_call(
        functools.partial(expand_kernel, width, height),
        grid=(channels // group,),
        out_shape=jax.ShapeDtypeStruct((channels * 9, positions), jnp.bfloat16),
        in_specs=[pl.BlockSpec((group, positions), lambda i: (i, 0))],
        out_specs=pl.BlockSpec((group * 9, positions), lambda i: (i, 0)),
        scratch_shapes=[pltpu.VMEM((positions // 128, group * 9, 128), jnp.float32)],
        cost_estimate=pl.CostEstimate(
            flops=channels * 9 * positions * 20,
            bytes_accessed=channels * positions * 20,
            transcendentals=0,
        ),
    )(image)


def update_kernel(width, height, new_share, image_ref, edge_ref, patches_ref, low_ref, side_ref, covariance_ref, *rest):
    out_ref, corners, gram, spread = rest[-4:]
    group, positions = image_ref.shape
    columns = covariance_ref.shape[1]
    tiles = -(-columns // 128)
    image = image_ref[...].astype(jnp.float32)
    place = lax.broadcasted_iota(jnp.int32, (1, positions), 1)
    column = place % width
    row = (place // width) % height
    row_ok = [row >= 1, None, row < height - 1]
    column_ok = [column >= 1, None, column < width - 1]
    planes = []
    for a, b in ((0, 0), (0, 2), (2, 0), (2, 2)):
        offset = (a - 1) * width + (b - 1)
        moved = pltpu.roll(image, (-offset) % positions, 1)
        planes.append(jnp.where(row_ok[a] & column_ok[b], moved, 0.0))
    corners[...] = jnp.concatenate(planes, axis=0).astype(jnp.bfloat16)
    contract = (((1,), (1,)), ((), ()))
    gram[0 : 4 * group, 128 : 128 + columns] = lax.dot_general(
        corners[...], patches_ref[...], contract, preferred_element_type=jnp.float32
    )
    size = low_ref.shape[1]
    edge = edge_ref[...].astype(jnp.float32)
    edge = [edge[:, k * size : k * size + size] for k in (0, 2, 3, 4, 5)]
    low = lax.dot_general(
        jnp.concatenate(edge[:2], axis=0).astype(jnp.bfloat16), low_ref[...], contract, preferred_element_type=jnp.float32
    )
    gram[4 * group : 6 * group, 128 : 128 + columns] = low
    side = lax.dot_general(
        jnp.concatenate(edge[2:], axis=0).astype(jnp.bfloat16), side_ref[...], contract, preferred_element_type=jnp.float32
    )
    gram[6 * group : 9 * group, 128 : 128 + columns] = side

    def shifted(plane, tile, by):
        near = gram[plane * group : plane * group + group, tile * 128 : tile * 128 + 384]
        return pltpu.roll(near, by % 384, 1)[:, 128:256]

    for tile in range(tiles):
        tap = (lax.broadcasted_iota(jnp.int32, (1, 128), 1) + tile * 128) % 9
        here = slice(128 + tile * 128, 256 + tile * 128)
        for b in range(2):
            mine = slice((4 + b) * group, (5 + b) * group)
            gram[mine, here] = gram[mine, here] + jnp.where(
                tap < 3, shifted(2 + b, tile, -3), shifted(b, tile, 3)
            )
    first = (0, 4, 2)
    for tile in range(tiles):
        lane = lax.broadcasted_iota(jnp.int32, (1, 128), 1) + tile * 128
        here = slice(128 + tile * 128, 256 + tile * 128)
        for a in range(3):
            left = first[a]
            middle = gram[(6 + a) * group : (7 + a) * group, here] + jnp.where(
                lane % 3 == 0, shifted(left + 1, tile, -1), shifted(left, tile, 1)
            )
            taps = (
                gram[left * group : (left + 1) * group, here],
                middle,
                gram[(left + 1) * group : (left + 2) * group, here],
            )
            for b in range(3):
                spread[tile, pl.ds(3 * a + b, group, stride=9), :] = taps[b]
        end = min(columns, tile * 128 + 128)
        cut = slice(tile * 128, end)
        out_ref[:, cut] = (
            decay_rate * covariance_ref[:, cut] + new_share * spread[tile][:, : end - tile * 128]
        )


def update(image, edges, patches, low, side, covariance, group, first, steps, slabs, so_far, width, height):
    channels, positions = image.shape
    columns = covariance.shape[1]
    each = covariance.shape[0] // (9 * group * slabs)
    padded = -(-columns // 128) * 128 + 256
    whole = lambda i: (0, 0)
    once = pl.Buffered(1)
    tile = pl.BlockSpec(
        (group * 9, columns), lambda i: ((i // steps) * each + first + i % steps, 0)
    )
    operands = [image, edges, patches, low, side, covariance]
    specs = [
        pl.BlockSpec((group, positions), lambda i: (i, 0)),
        pl.BlockSpec((group, edges.shape[1]), lambda i: (i, 0)),
        pl.BlockSpec(patches.shape, whole, pipeline_mode=once),
        pl.BlockSpec(low.shape, whole, pipeline_mode=once),
        pl.BlockSpec(side.shape, whole, pipeline_mode=once),
        tile,
    ]
    aliases = {}
    if so_far is not None:
        operands.append(so_far)
        specs.append(pl.BlockSpec(memory_space=pl.ANY))
        aliases = {6: 0}
    return pl.pallas_call(
        functools.partial(update_kernel, width, height, (1.0 - decay_rate) / positions),
        grid=(slabs * steps,),
        out_shape=jax.ShapeDtypeStruct(covariance.shape, jnp.float32),
        in_specs=specs,
        out_specs=tile,
        scratch_shapes=[
            pltpu.VMEM((4 * group, positions), jnp.bfloat16),
            pltpu.VMEM((9 * group, padded), jnp.float32),
            pltpu.VMEM((-(-columns // 128), group * 9, 128), jnp.float32),
        ],
        input_output_aliases=aliases,
        cost_estimate=pl.CostEstimate(
            flops=2 * 4 * channels * positions * columns,
            bytes_accessed=channels * 9 * columns * 8 + patches.size * 2,
            transcendentals=0,
        ),
        compiler_params=pltpu.CompilerParams(vmem_limit_bytes=62 * 1024 * 1024),
    )(*operands)


def edge_selector(batch, height, width):
    place = lax.broadcasted_iota(jnp.int32, (batch * height * width, 1), 0)
    parts = []
    for size, last, stride in ((width, (height - 1) * width, 1), (height, width - 1, width)):
        line = lax.broadcasted_iota(jnp.int32, (1, batch * size), 1)
        for k in (-1, 0, 1):
            at = line % size + k
            wanted = (line // size) * height * width + last + at * stride
            parts.append((place == wanted) & (at >= 0) & (at < size))
    return jnp.concatenate(parts, axis=1).astype(jnp.bfloat16)


def edge_values(image, selector):
    return lax.dot_general(
        image, selector, (((1,), (0,)), ((), ())), preferred_element_type=jnp.float32
    ).astype(jnp.bfloat16)


def interleave(planes):
    empty = jnp.zeros_like(next(iter(planes.values())))
    stacked = jnp.stack([planes.get(t, empty) for t in range(9)], axis=1)
    return stacked.reshape(-1, stacked.shape[2])


def plain(activations, covariance):
    wide_count = lax.axis_size("wide")
    narrow_count = lax.axis_size("narrow")
    repeats = narrow_count // wide_count
    batch, rows, width, channels = activations.shape
    height = rows * wide_count
    strip = jnp.transpose(activations.reshape(batch * rows * width, channels)).reshape(
        channels, batch, rows * width
    )
    moves = []
    for r in range(wide_count):
        for s in range(narrow_count):
            target = (s // repeats) * narrow_count + r + (s % repeats) * wide_count
            moves.append((r * narrow_count + s, target))
    row_strip = lax.ppermute(strip, ("wide", "narrow"), moves)
    group = max(g for g in range(8, 49, 8) if channels % g == 0)
    steps = channels // group
    cuts = [0, (steps * 2) // 5, steps] if steps > 3 else [0, steps]
    positions = batch * height * width
    column_strips = lax.all_gather(strip, "wide")
    row_parts = []
    for low_cut, high_cut in zip(cuts[:-1], cuts[1:]):
        piece = row_strip[low_cut * group : high_cut * group]
        if row_parts:
            piece, row_parts[-1] = lax.optimization_barrier((piece, row_parts[-1]))
        row_parts.append(lax.all_gather(piece, "narrow"))
    selector = edge_selector(batch, height, width)
    column_image = jnp.transpose(column_strips, (1, 2, 0, 3)).reshape(channels, positions)
    patches = expand(column_image, width, height)
    edges = edge_values(column_image, selector)
    size = edges.shape[1] // 6
    edge = [edges[:, k * size : k * size + size] for k in range(6)]
    low = interleave({3 + b: edge[b] for b in range(3)})
    side = interleave({3 * a + 1: edge[3 + a] for a in range(3)})
    updated = None
    for part, first in enumerate(cuts[:-1]):
        count = cuts[part + 1] - first
        own = count * group
        image = jnp.transpose(
            row_parts[part].reshape(repeats, wide_count, own, batch, rows * width), (0, 2, 3, 1, 4)
        ).reshape(repeats * own, positions)
        edges = edge_values(image, selector)
        updated = update(
            image, edges, patches, low, side, covariance, group, first, count, repeats, updated, width, height
        )
    return updated


MESH = pl.DeviceIdType.MESH


def expand_group(channels):
    return max(g for g in (16, 32, 48) if channels % g == 0)


def roll_taps(image, width, height):
    positions = image.shape[1]
    place = lax.broadcasted_iota(jnp.int32, (8, positions), 1)
    column = place % width
    row = (place // width) % height
    return [row >= 1, None, row < height - 1], [column >= 1, None, column < width - 1]


def gather_kernel(shape, own_ref, row_ref, patches_ref, low_ref, side_ref, sel_ref, *rest):
    (
        col, spread, staged, sel, edges, line,
        own_send, own_recv, pass_send, row_send, row_recv, local, out_sem,
    ) = rest
    width, height, wide, narrow, inner = shape
    repeats, _, batch, channels, lanes = row_ref.shape
    outer = narrow // inner
    pairs = wide // 2
    r = lax.axis_index("wide")
    s = lax.axis_index("narrow")
    z, y = s // inner, s % inner
    pair, core = r // 2, r % 2
    sibling = pair * 2 + 1 - core
    others = [((pair + p) % pairs) * 2 + core for p in range(1, pairs)]
    steps = ((z + 1 < outer, z + 1, y), (z > 0, z - 1, y), (y + 1 < inner, z, y + 1), (y > 0, z, y - 1))

    barrier = pltpu.get_barrier_semaphore()
    for q in [sibling] + others:
        pl.semaphore_signal(barrier, inc=1, device_id=(q, s), device_id_type=MESH)
    for there, to_z, to_y in steps:

        @pl.when(there)
        def _(to_z=to_z, to_y=to_y):
            pl.semaphore_signal(barrier, inc=1, device_id=(r, to_z * inner + to_y), device_id_type=MESH)

    greeted = pairs
    for there, _, _ in steps:
        greeted = greeted + jnp.where(there, 1, 0)
    pl.semaphore_wait(barrier, greeted)

    def to_core(source, strip, b, q, send):
        return pltpu.make_async_remote_copy(
            src_ref=source,
            dst_ref=col.at[strip, b],
            send_sem=send,
            recv_sem=own_recv.at[strip, b],
            device_id=(q, s),
            device_id_type=MESH,
        )

    def first_sends(b):
        return [to_core(own_ref.at[b], r, b, q, own_send.at[n, b]) for n, q in enumerate([sibling] + others)]

    for b in range(batch):
        for copy in first_sends(b):
            copy.start()
    mine = pltpu.make_async_copy(own_ref, col.at[r], local.at[repeats])
    mine.start()

    order = [r, sibling]
    for q in others:
        order += [q, (q // 2) * 2 + 1 - core]

    streams = []
    for k in range(repeats):
        source = r * repeats + k
        from_z, from_y = source // inner, source % inner
        on = y == from_y
        children = (
            (steps[0][0] & on & (z >= from_z), steps[0]),
            (steps[1][0] & on & (z <= from_z), steps[1]),
            (steps[2][0] & (y >= from_y), steps[2]),
            (steps[3][0] & (y <= from_y), steps[3]),
        )
        any_child = children[0][0] | children[1][0] | children[2][0] | children[3][0]
        streams.append((s == source, any_child, children))

    cut = -(-channels // 32) * 16
    halves = (pl.ds(0, cut), pl.ds(cut, channels - cut))

    def onward(k, j, b, h, source):
        for n, (there, (_, to_z, to_y)) in enumerate(streams[k][2]):

            @pl.when(there)
            def _(n=n, to_z=to_z, to_y=to_y):
                pltpu.make_async_remote_copy(
                    src_ref=source.at[halves[h]],
                    dst_ref=row_ref.at[k, order[j], b, halves[h]],
                    send_sem=row_send.at[k, n],
                    recv_sem=row_recv.at[k, j, b, h],
                    device_id=(r, to_z * inner + to_y),
                    device_id_type=MESH,
                ).start()

    def landed(k, j, b, h):
        ref = row_ref.at[k, order[j], b, halves[h]]
        pltpu.make_async_copy(ref, ref, row_recv.at[k, j, b, h]).wait()

    def passed(p, b):
        strip = order[2 * p]
        return to_core(col.at[strip, b], strip, b, sibling, pass_send.at[p - 1, b])

    group = expand_group(channels)
    rows = group * 9
    expansions = channels // group
    block = height * width
    positions = batch * block
    lines = batch * height
    line[...] = jnp.zeros_like(line)
    for ref in (low_ref, side_ref):
        ref[channels * 9 :, :] = jnp.zeros((ref.shape[0] - channels * 9, ref.shape[1]), jnp.bfloat16)

    def written(e, b, slot):
        top = pl.multiple_of(e * rows, 16)
        left = pl.multiple_of(b * block, 128)
        return pltpu.make_async_copy(
            staged.at[slot], patches_ref.at[pl.ds(top, rows), pl.ds(left, block)], out_sem.at[slot]
        )

    def expand_step(e, b):
        turn = b * expansions + e
        slot = turn % 2

        @pl.when(turn >= 2)
        def _():
            written(0, 0, slot).wait()

        first = pl.multiple_of(e * group, 16)
        image = jnp.concatenate([col[w, b, pl.ds(first, group), :] for w in range(wide)], axis=1).astype(jnp.float32)
        row_ok, column_ok = roll_taps(image, width, height)
        for a in range(3):
            for c in range(3):
                offset = (a - 1) * width + (c - 1)
                moved = pltpu.roll(image, (-offset) % block, 1) if offset else image
                keep = row_ok[a]
                if column_ok[c] is not None:
                    keep = column_ok[c] if keep is None else keep & column_ok[c]
                for half in range(group // 8):
                    part = moved[half * 8 : half * 8 + 8]
                    if keep is not None:
                        part = jnp.where(keep, part, 0.0)
                    for tile in range(block // 128):
                        spread[tile, pl.ds(half * 72 + 3 * a + c, 8, stride=9), :] = part[
                            :, tile * 128 : tile * 128 + 128
                        ]
        for tile in range(block // 128):
            staged[slot, :, tile * 128 : tile * 128 + 128] = spread[tile].astype(jnp.bfloat16)
        written(e, b, slot).start()

    mine.wait()
    sel_copy = pltpu.make_async_copy(sel, sel_ref, local.at[repeats + 1])

    def select():
        at = lax.broadcasted_iota(jnp.int32, (1, positions), 1)
        across = lax.broadcasted_iota(jnp.int32, (batch * width, 1), 0)
        down = lax.broadcasted_iota(jnp.int32, (lines, 1), 0)
        low_at = (across // width) * block + (height - 1) * width + across % width
        side_at = (down // height) * block + (down % height) * width + width - 1
        for n, wanted in enumerate((low_at, side_at)):
            sel[n * batch * width : n * batch * width + wanted.shape[0], :] = (
                (at == wanted).astype(jnp.float32).astype(jnp.bfloat16)
            )
        sel_copy.start()

    def turn(b, _):
        for j in range(wide):
            if j > 0:
                to_core(col.at[order[j], b], order[j], b, sibling, own_send.at[0, b]).wait_recv()
            if j > 1 and j % 2 == 0:
                passed(j // 2, b).start()
            for k in range(repeats):

                @pl.when(streams[k][0])
                def _(k=k):
                    for h in range(2):
                        onward(k, j, b, h, col.at[order[j], b])

        pl.when(b == 0)(select)
        for j in range(wide):
            for h in range(2):
                for k in range(repeats):

                    @pl.when(jnp.logical_not(streams[k][0]) & streams[k][1])
                    def _(k=k, h=h):
                        landed(k, j, b, h)
                        onward(k, j, b, h, row_ref.at[k, order[j], b])

                slot = 2 * j + h
                lax.fori_loop(
                    slot * expansions // (2 * wide),
                    (slot + 1) * expansions // (2 * wide),
                    lambda e, _: (expand_step(e, b), 0)[1],
                    0,
                )

        return 0

    lax.fori_loop(0, batch, turn, 0)
    for k in range(repeats):

        @pl.when(streams[k][0])
        def _(k=k):
            pltpu.make_async_copy(col, row_ref.at[k], local.at[k]).start()

    pieces = [col[w, n] for n in range(batch) for w in range(wide)]
    edges[...] = lax.dot_general(
        jnp.concatenate(pieces, axis=1), sel[...], (((1,), (1,)), ((), ())), preferred_element_type=jnp.float32
    )

    def edge_step(e, _):
        first = pl.multiple_of(e * 16, 16)
        edge = edges[pl.ds(first, 16), :]
        for n, (size, base, stride) in enumerate(((width, 3, 1), (height, 1, 3))):
            count = batch * size
            value = edge[:, n * batch * width : n * batch * width + count]
            spot = lax.broadcasted_iota(jnp.int32, (16, count), 1) % size
            for k in (-1, 0, 1):
                moved = pltpu.roll(value, (-k) % count, 1) if k else value
                moved = jnp.where((spot + k >= 0) & (spot + k < size), moved, 0.0)
                for half in range(16 // 8):
                    line[n, pl.ds(half * 72 + base + (k + 1) * stride, 8, stride=9), :] = moved[
                        half * 8 : half * 8 + 8
                    ]
        top = pl.multiple_of(e * 144, 16)
        low_ref[pl.ds(top, 144), :] = line[0].astype(jnp.bfloat16)
        side_ref[pl.ds(top, 144), :] = line[1].astype(jnp.bfloat16)
        return 0

    lax.fori_loop(0, channels // 16, edge_step, 0)
    for k in range(repeats):

        @pl.when(jnp.logical_not(streams[k][0]) & jnp.logical_not(streams[k][1]))
        def _(k=k):
            for b in range(batch):
                for j in range(wide):
                    for h in range(2):
                        landed(k, j, b, h)

    for slot in range(min(2, batch * expansions)):
        written(0, 0, slot).wait()
    sel_copy.wait()
    for b in range(batch):
        for copy in first_sends(b):
            copy.wait_send()
        for p in range(1, pairs):
            passed(p, b).wait_send()
    for k in range(repeats):
        for n, (there, _) in enumerate(streams[k][2]):

            @pl.when(there)
            def _(k=k, n=n):
                pltpu.make_async_copy(row_ref.at[k], row_ref.at[k], row_send.at[k, n]).wait()

        @pl.when(streams[k][0])
        def _(k=k):
            pltpu.make_async_copy(col, row_ref.at[k], local.at[k]).wait()


def gather(own, wide, narrow, width, height):
    batch, channels, lanes = own.shape
    repeats = narrow // wide
    inner = max(d for d in range(1, narrow + 1) if narrow % d == 0 and d * d <= narrow)
    positions = batch * wide * lanes
    lines = batch * (width + height)
    padded = padded_columns(channels * 9)
    anywhere = pl.BlockSpec(memory_space=pl.ANY)
    vmem = pl.BlockSpec(memory_space=pltpu.VMEM)
    bf16 = jnp.bfloat16
    return pl.pallas_call(
        functools.partial(gather_kernel, (width, height, wide, narrow, inner)),
        out_shape=[
            jax.ShapeDtypeStruct((repeats, wide, batch, channels, lanes), bf16),
            jax.ShapeDtypeStruct((channels * 9, positions), bf16),
            jax.ShapeDtypeStruct((padded, batch * width), bf16),
            jax.ShapeDtypeStruct((padded, batch * height), bf16),
            jax.ShapeDtypeStruct((lines, positions), bf16),
        ],
        in_specs=[vmem],
        out_specs=[anywhere, anywhere, vmem, vmem, anywhere],
        scratch_shapes=[
            pltpu.VMEM((wide, batch, channels, lanes), bf16),
            pltpu.VMEM((wide * lanes // 128, expand_group(channels) * 9, 128), jnp.float32),
            pltpu.VMEM((2, expand_group(channels) * 9, wide * lanes), bf16),
            pltpu.VMEM((lines, positions), bf16),
            pltpu.VMEM((channels, lines), jnp.float32),
            pltpu.VMEM((2, 144, batch * width), jnp.float32),
            pltpu.SemaphoreType.DMA((wide // 2, batch)),
            pltpu.SemaphoreType.DMA((wide, batch)),
            pltpu.SemaphoreType.DMA((max(1, wide // 2 - 1), batch)),
            pltpu.SemaphoreType.DMA((repeats, 4)),
            pltpu.SemaphoreType.DMA((repeats, wide, batch, 2)),
            pltpu.SemaphoreType.DMA((repeats + 2,)),
            pltpu.SemaphoreType.DMA((2,)),
        ],
        compiler_params=pltpu.CompilerParams(
            collective_id=0, has_side_effects=True, vmem_limit_bytes=60 * 1024 * 1024
        ),
    )(own)


parts = 3


def padded_columns(columns):
    return -(-columns // (256 * parts)) * 256 * parts


def combine_kernel(
    width, height, new_share, row_ref, low_ref, side_ref, sel_ref, patches_ref, covariance_ref, out_ref,
    patches, edges, corners, low_rows, side_rows, even, odd, rolled, spread, fetched,
):
    repeats, wide, batch, channels, lanes = row_ref.shape
    positions = wide * batch * lanes
    group = corners.shape[0] // 4
    steps = channels // group
    groups = repeats * steps
    sub = group // parts
    columns = covariance_ref.shape[1]
    tiles = -(-columns // 128)
    chunk = patches.shape[0] // parts
    at = pl.program_id(0)
    i, j = at // parts, at % parts
    size = low_ref.shape[1]
    lines = sel_ref.shape[0]
    contract = (((1,), (1,)), ((), ()))

    pieces = [n for n in range(parts) if n * chunk < columns]

    def fetch(n):
        rows = pl.ds(n * chunk, min(chunk, columns - n * chunk))
        return pltpu.make_async_copy(patches_ref.at[rows, :], patches.at[rows, :], fetched.at[n])

    selector = pltpu.make_async_copy(sel_ref, corners.at[pl.ds(0, lines), :], fetched.at[parts])

    @pl.when(at == 0)
    def _():
        selector.start()
        for n in pieces:
            fetch(n).start()
        patches[columns:, :] = jnp.zeros((patches.shape[0] - columns, positions), jnp.bfloat16)
        selector.wait()
        for k in range(repeats):
            whole = jnp.concatenate([row_ref[k, w, n] for n in range(batch) for w in range(wide)], axis=1)
            edges[k] = lax.dot_general(whole, corners[0:lines, :], contract, preferred_element_type=jnp.float32)

    def edge_taps(value, length, taps):
        count = value.shape[1]
        spot = lax.broadcasted_iota(jnp.int32, value.shape, 1) % length
        out = []
        for by in taps:
            moved = pltpu.roll(value, (-by) % count, 1) if by else value
            out.append(jnp.where((spot + by >= 0) & (spot + by < length), moved, 0.0))
        return jnp.concatenate(out, axis=0).astype(jnp.bfloat16)

    @pl.when((j == 0) & (i < groups))
    def _():
        k = i // steps
        first = pl.multiple_of((i % steps) * group, 8)
        image = jnp.concatenate(
            [row_ref[k, w, n, pl.ds(first, group), :] for n in range(batch) for w in range(wide)], axis=1
        ).astype(jnp.float32)
        place = lax.broadcasted_iota(jnp.int32, (1, positions), 1)
        column = place % width
        row = (place // width) % height
        row_ok = [row >= 1, None, row < height - 1]
        column_ok = [column >= 1, None, column < width - 1]
        for n, (a, b) in enumerate(((0, 0), (0, 2), (2, 0), (2, 2))):
            offset = (a - 1) * width + (b - 1)
            moved = pltpu.roll(image, (-offset) % positions, 1)
            moved = jnp.where(row_ok[a] & column_ok[b], moved, 0.0)
            corners[n * group : n * group + group, :] = moved.astype(jnp.bfloat16)
        edge = edges[k, pl.ds(first, group), :]
        low_rows[...] = edge_taps(edge[:, :size], width, (-1, 1))
        side_rows[...] = edge_taps(edge[:, size:], height, (-1, 0, 1))

    for n in pieces:

        @pl.when(at == n)
        def _(n=n):
            fetch(n).wait()

    def multiply(gram):
        for piece in range(chunk // 256):
            start = pl.multiple_of(j * chunk + piece * 256, 256)
            here = pl.ds(pl.multiple_of(128 + start, 128), 256)
            rows = pl.ds(start, 256)
            for left, right, top, count in (
                (corners, patches, 0, 4),
                (low_rows, low_ref, 4, 2),
                (side_rows, side_ref, 6, 3),
            ):
                gram[top * group : (top + count) * group, here] = lax.dot_general(
                    left[...], right[rows, :], contract, preferred_element_type=jnp.float32
                )

    lane = lax.broadcasted_iota(jnp.int32, (8, 128), 1)

    def finish(gram):
        def rows_of(p, n):
            return pl.ds(pl.multiple_of(p * group + j * sub + n * 8, 8), 8)

        def place(tile):
            return slice(128 + tile * 128, 256 + tile * 128)

        def roll_all(n, wanted):
            for q, p, by in wanted:
                rolled[n % 2, q] = pltpu.roll(gram[rows_of(p, n), 128 : 128 + tiles * 128], by % (tiles * 128), 1)

        def moved(n, q, tile):
            return rolled[n % 2, q, :, tile * 128 : tile * 128 + 128]

        def corner_rolls(n):
            roll_all(n, ((0, 0, 3), (1, 1, 3), (2, 2, -3), (3, 3, -3), (4, 0, 1), (5, 1, -1), (8, 2, 1), (9, 3, -1)))

        def middle_rows(n):
            for tile in range(tiles):
                upper = (lane + tile * 128) % 9 < 3
                for b in range(2):
                    gram[rows_of(4 + b, n), place(tile)] = gram[rows_of(4 + b, n), place(tile)] + jnp.where(
                        upper, moved(n, 2 + b, tile), moved(n, b, tile)
                    )

        def middle_rolls(n):
            roll_all(n, ((6, 4, 1), (7, 5, -1)))

        def write(n):
            for tile in range(tiles):
                first = (lane + tile * 128) % 3 == 0
                for a, left in enumerate((0, 4, 2)):
                    middle = gram[rows_of(6 + a, n), place(tile)] + jnp.where(
                        first, moved(n, 5 + 2 * a, tile), moved(n, 4 + 2 * a, tile)
                    )
                    taps = (gram[rows_of(left, n), place(tile)], middle, gram[rows_of(left + 1, n), place(tile)])
                    for b in range(3):
                        spread[tile % 4, pl.ds(3 * a + b, 8, stride=9), :] = taps[b]
                end = min(columns, tile * 128 + 128)
                cut = slice(tile * 128, end)
                rows = slice(n * 72, n * 72 + 72)
                out_ref[rows, cut] = (
                    decay_rate * covariance_ref[rows, cut]
                    + new_share * spread[tile % 4][:, : end - tile * 128]
                )

        slabs = sub // 8
        corner_rolls(0)
        for n in range(slabs):
            middle_rows(n)
            middle_rolls(n)
            if n + 1 < slabs:
                corner_rolls(n + 1)
            write(n)

    pair = (even, odd)

    @pl.when(i == 0)
    def _():
        multiply(pair[0])

    for parity in range(2):

        @pl.when((i > 0) & (i < groups) & (i % 2 == parity))
        def _(parity=parity):
            multiply(pair[parity])
            finish(pair[1 - parity])

    @pl.when(i == groups)
    def _():
        finish(pair[(groups - 1) % 2])


def combine(row, patches, low, side, sel, covariance, width, height):
    repeats, wide, batch, channels, lanes = row.shape
    positions = wide * batch * lanes
    columns = covariance.shape[1]
    unit = 8 * parts
    group = max(g for g in range(unit, 121, unit) if channels % g == 0)
    groups = repeats * channels // group
    padded = low.shape[0]
    once = pl.Buffered(1)

    def resident(array):
        return pl.BlockSpec(array.shape, lambda t: (0,) * array.ndim, pipeline_mode=once)

    anywhere = pl.BlockSpec(memory_space=pl.ANY)
    tile = pl.BlockSpec((group // parts * 9, columns), lambda t: (jnp.maximum(t - parts, 0), 0))
    return pl.pallas_call(
        functools.partial(combine_kernel, width, height, (1.0 - decay_rate) / positions),
        grid=((groups + 1) * parts,),
        out_shape=jax.ShapeDtypeStruct(covariance.shape, jnp.float32),
        in_specs=[resident(row), resident(low), resident(side), anywhere, anywhere, tile],
        out_specs=tile,
        scratch_shapes=[
            pltpu.VMEM((padded, positions), jnp.bfloat16),
            pltpu.VMEM((repeats, channels, sel.shape[0]), jnp.float32),
            pltpu.VMEM((4 * group, positions), jnp.bfloat16),
            pltpu.VMEM((2 * group, low.shape[1]), jnp.bfloat16),
            pltpu.VMEM((3 * group, side.shape[1]), jnp.bfloat16),
            pltpu.VMEM((9 * group, 128 + padded), jnp.float32),
            pltpu.VMEM((9 * group, 128 + padded), jnp.float32),
            pltpu.VMEM((2, 10, 8, -(-columns // 128) * 128), jnp.float32),
            pltpu.VMEM((4, 72, 128), jnp.float32),
            pltpu.SemaphoreType.DMA((parts + 1,)),
        ],
        cost_estimate=pl.CostEstimate(
            flops=2 * 4 * repeats * channels * positions * columns,
            bytes_accessed=covariance.size * 8 + patches.size * 2,
            transcendentals=0,
        ),
        compiler_params=pltpu.CompilerParams(vmem_limit_bytes=67043328),
    )(row, low, side, sel, patches, covariance)


def shards(activations, covariance):
    wide = lax.axis_size("wide")
    narrow = lax.axis_size("narrow")
    batch, rows, width, channels = activations.shape
    height = rows * wide
    lanes = rows * width
    if lanes % 128 or channels % 16 or wide % 2 or narrow % wide or width != height:
        return plain(activations, covariance)
    own = jnp.transpose(activations.reshape(batch, lanes, channels), (0, 2, 1))
    row, patches, low, side, sel = gather(own, wide, narrow, width, height)
    return combine(row, patches, low, side, sel, covariance, width, height)


def solution(mesh):
    return jax.shard_map(
        shards,
        mesh=mesh,
        in_specs=(P(None, "wide", None, "narrow"), P("wide", "narrow")),
        out_specs=P("wide", "narrow"),
        check_vma=False,
    )
```
